32 devices in a mesh: op: 4 (over y, x), str: 8 (over z, core).
Axes of the slice: x: 2, y: 2, z: 4, core: 2. Of those that a mesh axis runs over, the one named last changes fastest.
Arguments:
- coeffs: float32 [4096, 4096], P('str'), may hold values from -6 to 6
- previous: float32 [4096, 4096], P('str'), may hold values from -6 to 6
- block_values: bfloat16 [4, 32, 6, 128, 128], P('op'), may hold values from -0.21875 to 0.21875
- block_cols: int32 [4, 32, 6], P('op'), may hold values from 0 to 31, as said below
Outputs:
- advanced: float32 [4096, 4096], P('str')
The draws below stay inside these ranges and needn't reach their ends.
Inputs may be any that keep to these rules, and one draw needn't show every extreme that they name: For every term k and block row r, block_cols[k, r, 0] equals r and the 6 entries of block_cols[k, r] are distinct.
All inputs are finite; a program needn't handle non-finite values.
Results may differ from the reference program's by a relative error of at most 0.0003.
Values sent between devices are 32-bit elements; how exact they have to be, the bound alone decides.
A program may use at most 192 MiB of HBM per device.

```python
import math
import jax
import jax.numpy as jnp
from jax import lax

STRINGS = 4096
BLOCK = 128
BLOCKS = 32
ROW_BLOCKS = 6
TERMS = 4
STEPS = 2


def draw_block_cols(key, part):
    row_keys = jax.random.split(key, TERMS * BLOCKS)

    def one_row(row_key):
        return jax.random.permutation(row_key, BLOCKS - 1)[:ROW_BLOCKS - 1].astype(jnp.int32)
    others = jax.vmap(one_row)(row_keys).reshape(TERMS, BLOCKS, ROW_BLOCKS - 1)
    block_rows = jnp.arange(BLOCKS, dtype=jnp.int32)[None, :, None]
    others = (block_rows + 1 + others) % BLOCKS
    diagonal = jnp.broadcast_to(block_rows, (TERMS, BLOCKS, 1))
    return jnp.concatenate([diagonal, others], axis=2).astype(jnp.int32)


def shard_levels(rng, extent, shards, smallest, top_value):
    gain, own = 1.0, jax.random.fold_in(rng, 6)
    for dim, parts in shards:
        steps = jnp.exp(jax.random.uniform(jax.random.fold_in(own, dim), (parts,), jnp.float32, smallest / len(shards), top_value / len(shards)))
        gain = gain * jnp.repeat(steps, extent[dim] // parts).reshape([-1 if axis == dim else 1 for axis in range(len(extent))])
    return gain


def bell_draw(rng, extent, scale, most, pieces=(), held_as=jnp.bfloat16):
    gain = shard_levels(rng, extent, pieces, -0.22, 0.18) if pieces else 1.0
    drawn = jax.random.normal(rng, extent, jnp.float32) * scale * gain
    return jnp.minimum(jnp.maximum(drawn, -most), most).astype(held_as)


def setup_inputs(seed: int = 0) -> dict:
    arg_keys = jax.random.split(jax.random.key(seed), 5)
    return {
        "coeffs": bell_draw(arg_keys[0], (STRINGS, STRINGS), 1.0, 6.0, ((0, 8),), jnp.float32),
        "previous": bell_draw(arg_keys[1], (STRINGS, STRINGS), 1.0, 6.0, ((0, 8),), jnp.float32),
        "block_values": bell_draw(arg_keys[2], (TERMS, BLOCKS, ROW_BLOCKS, BLOCK, BLOCK), (ROW_BLOCKS * BLOCK) ** -0.5, 0.21875, ((0, 4),)),
        "block_cols": draw_block_cols(jax.random.fold_in(arg_keys[4], 71), 0),
    }


def apply_term(field, values, columns):
    factors = values.astype(jnp.float32)
    column_list = columns.reshape(-1)
    gathered = jnp.take(field.reshape(STRINGS, BLOCKS, BLOCK), column_list, axis=1)
    gathered = gathered.reshape(STRINGS, BLOCKS, ROW_BLOCKS, BLOCK)
    beta_side = jnp.einsum('arjc,rjoc->aro', gathered, factors, precision=lax.Precision.HIGHEST)
    beta_side = beta_side.reshape(STRINGS, STRINGS)
    grouped = jnp.take(beta_side.reshape(BLOCKS, BLOCK, STRINGS), column_list, axis=0)
    grouped = grouped.reshape(BLOCKS, ROW_BLOCKS, BLOCK, STRINGS)
    alpha_side = jnp.einsum('rjoc,rjcb->rob', factors, grouped, precision=lax.Precision.HIGHEST)
    return alpha_side.reshape(STRINGS, STRINGS)

def sigma_all(field, block_values, block_cols):

    def add_term(summed, term_pair):
        return (summed + apply_term(field, term_pair[0], term_pair[1]), None)
    summed, unused = lax.scan(add_term, jnp.zeros((STRINGS, STRINGS), jnp.float32), (block_values, block_cols))
    return summed

def reference(coeffs, previous, block_values, block_cols):
    step_scale = 2.0 / math.sqrt(TERMS)
    earlier, current = (previous, coeffs)
    for step_index in range(STEPS):
        updated = step_scale * sigma_all(current, block_values, block_cols) - earlier
        earlier, current = (current, updated)
    return current
```

```python
import functools
import math

import jax
import jax.numpy as jnp
from jax import lax
from jax.experimental import pallas as pl
from jax.experimental.pallas import tpu as pltpu
from jax.sharding import PartitionSpec as P

F32, BF16 = jnp.float32, jnp.bfloat16
VMEM_LIMIT = 67_043_328


def split(x):
    high = x.astype(BF16)
    return high, (x - high.astype(F32)).astype(BF16)


def flip(a, b, size):
    total, bit = 0, 1
    while bit < size:
        total = total + bit * lax.rem(lax.div(a, bit) + lax.div(b, bit), 2)
        bit *= 2
    return total


def body(
    shards, op_size, slots, block, chunks, scale,
    cols_ref, a_hbm, v_hbm, p_hbm, out_hbm,
    a_ref, field, ysend, yrecv, wrecv, small, part, ufull, rsrecv, vstage, vq,
    a_sem, v_sem, p_sem, q_sem, o_sem,
    y_send, y_recv, r1_send, r1_recv, g1_send, g1_recv,
    w_send, w_recv, r2_send, r2_recv, g2_send, g2_recv,
):
    blocks = chunks * shards
    rows = chunks * block
    piece = rows // op_size
    thin = min(block, piece)
    wide = rows
    share = blocks // op_size
    early = max(1, chunks // 2)
    i32 = jnp.int32
    me, op = lax.axis_index("str").astype(i32), lax.axis_index("op").astype(i32)

    def peer(d):
        return flip(me, jnp.asarray(d, i32), shards)

    def mate(q):
        return flip(op, jnp.asarray(q, i32), op_size)

    def wait(ref, sem):
        pltpu.make_async_copy(ref, ref, sem).wait()

    def to_peer(src, dst, send, recv, d):
        pltpu.make_async_remote_copy(
            src_ref=src, dst_ref=dst, send_sem=send, recv_sem=recv,
            device_id={"str": peer(d)}, device_id_type=pl.DeviceIdType.MESH,
        ).start()

    def to_mate(src, dst, send, recv, q):
        pltpu.make_async_remote_copy(
            src_ref=src, dst_ref=dst, send_sem=send, recv_sem=recv,
            device_id={"op": mate(q)}, device_id_type=pl.DeviceIdType.MESH,
        ).start()

    def loop(n, start=0):
        def run(step):
            lax.fori_loop(start, n, lambda i, _: (step(i), None)[1], None)
        return run

    def v_copy(g):
        return pltpu.make_async_copy(
            v_hbm.at[:, pl.ds(pl.multiple_of(g * wide, block), wide)],
            vstage.at[lax.rem(g, 2)],
            v_sem.at[lax.rem(g, 2)],
        )

    a_copy = pltpu.make_async_copy(a_hbm, a_ref, a_sem)
    quarter = pl.ds(pl.multiple_of(op * (share * block), block), share * block)
    q_copy = pltpu.make_async_copy(v_hbm.at[:, quarter], vq, q_sem)

    v_copy(jnp.int32(0)).start()
    a_copy.start()

    barrier = pltpu.get_barrier_semaphore()
    for d in range(1, shards):
        pl.semaphore_signal(
            barrier, inc=1, device_id={"str": peer(d)}, device_id_type=pl.DeviceIdType.MESH
        )
    for q in range(1, op_size):
        pl.semaphore_signal(
            barrier, inc=1, device_id={"op": mate(q)}, device_id_type=pl.DeviceIdType.MESH
        )

    @loop(shards * chunks)
    def _(i):
        d, c = lax.div(i, chunks), lax.rem(i, chunks)
        at = pl.multiple_of((peer(d) * chunks + c) * block, block)
        pltpu.make_async_copy(
            p_hbm.at[pl.ds(pl.multiple_of(op * piece, piece), piece), pl.ds(at, block)],
            ysend.at[c, d, pl.ds(rows, piece)],
            p_sem,
        ).start()

    @loop(shards)
    def _(g):
        @pl.when(g + 1 < shards)
        def _():
            v_copy(g + 1).start()

        v_copy(g).wait()
        for i in range(chunks):
            high, low = split(vstage[lax.rem(g, 2), :, i * block : (i + 1) * block])
            field[g * chunks + i, :rows] = high
            field[g * chunks + i, rows:] = low

    q_copy.start()
    a_copy.wait()
    wait(ysend.at[:, :, pl.ds(rows, piece)], p_sem)
    pl.semaphore_wait(barrier, shards - 1 + op_size - 1)

    def operator_row(row):
        return jnp.concatenate([a_ref[row, j] for j in range(slots)], axis=1)

    def beta(source, row, m):
        left = jnp.concatenate(
            [source[cols_ref[row * slots + j]] for j in range(slots)], axis=1
        )
        both = lax.dot_general(
            left, operator_row(row), (((1,), (1,)), ((), ())), preferred_element_type=F32
        )
        return both[:m] + both[m:]

    def alpha(load, row):
        right = jnp.concatenate(
            [
                jnp.concatenate(load(cols_ref[row * slots + j]), axis=1)
                for j in range(slots)
            ],
            axis=0,
        )
        both = jnp.dot(operator_row(row), right, preferred_element_type=F32)
        return both[:, :block] + both[:, block:]

    @loop(shards * chunks)
    def _(i):
        c, d = lax.div(i, shards), lax.rem(i, shards)
        ysend[c, d, :rows] = beta(field, peer(d) * chunks + c, rows)

        @pl.when(d > 0)
        def _():
            to_peer(ysend.at[c, d], yrecv.at[c, d - 1], y_send.at[c], y_recv.at[c], d)

    def keep(at_block, x):
        high, low = split(x)
        small[at_block, :block] = high
        small[at_block, block:] = low

    def pieces(h):
        for t in range(block // thin):
            g = h * block + t * thin
            yield g // piece, g % piece, t * thin

    def alpha_first(c):
        slot = lax.rem(c, 2)
        wait(yrecv.at[c], y_recv.at[c])
        for h in range(chunks):
            keep(me * chunks + h, ysend[c, 0, h * block : (h + 1) * block])

        @loop(shards, 1)
        def _(d):
            for h in range(chunks):
                keep(peer(d) * chunks + h, yrecv[c, d - 1, h * block : (h + 1) * block])

        @pl.when(c >= 2)
        def _():
            wait(rsrecv.at[c - 2], r1_send.at[c - 2])

        @loop(shards)
        def _(d):
            for h in range(chunks):
                value = scale * alpha(
                    lambda b: [small[b, :block], small[b, block:]], peer(d) * chunks + h
                )
                for owner, at, start in pieces(h):
                    here = pl.ds(pl.multiple_of(d * piece + at, thin), thin)
                    part[slot, mate(owner), here] = value[start : start + thin]

        for q in range(1, op_size):
            to_mate(
                part.at[slot, q], rsrecv.at[c, q - 1], r1_send.at[c], r1_recv.at[c], q
            )

    def add_first(c):
        slot = lax.rem(c, 2)
        wait(rsrecv.at[c], r1_recv.at[c])

        @pl.when(c >= 2)
        def _():
            wait(ufull.at[0, pl.ds(1, op_size - 1)], g1_send.at[c - 2])

        def one(d, earlier):
            here = pl.ds(pl.multiple_of(d * piece, piece), piece)
            total = part[slot, 0, here]
            for q in range(1, op_size):
                total = total + rsrecv[c, q - 1, here]
            ufull[slot, 0, here] = total - earlier

        one(0, ysend[c, 0, rows:])

        @loop(shards, 1)
        def _(d):
            one(d, yrecv[c, d - 1, rows:])

        for q in range(1, op_size):
            to_mate(
                ufull.at[slot, 0], ufull.at[slot, q], g1_send.at[c], g1_recv.at[c], q
            )

    def alpha_piece(r, c):
        at = pl.multiple_of(r * block, block)
        column = pl.multiple_of(2 * block * c, 2 * block)

        @loop(shards)
        def _(d):
            ysend[c, d, pl.ds(at, block)] = alpha(
                lambda b: [
                    field[b, pl.ds(column, block)],
                    field[b, pl.ds(column + block, block)],
                ],
                peer(d) * chunks + r,
            )

            @pl.when(d > 0)
            def _():
                to_peer(
                    ysend.at[c, d, pl.ds(at, block)], wrecv.at[r, c, d - 1],
                    w_send.at[r], w_recv.at[r], d,
                )

    def alpha_second(c):
        slot = lax.rem(c, 2)
        wait(ufull.at[slot, pl.ds(1, op_size - 1)], g1_recv.at[c])
        column = pl.multiple_of(2 * block * c, 2 * block)

        @loop(shards)
        def _(d):
            for h in range(chunks):
                x = jnp.concatenate(
                    [
                        ufull[slot, mate(owner), pl.ds(pl.multiple_of(d * piece + at, thin), thin)]
                        for owner, at, _ in pieces(h)
                    ],
                    axis=0,
                )
                high, low = split(x)
                field[peer(d) * chunks + h, pl.ds(column, block)] = high
                field[peer(d) * chunks + h, pl.ds(column + block, block)] = low

        wait(yrecv.at[c], y_send.at[c])

        @loop(early)
        def _(r):
            alpha_piece(r, c)

    @loop(chunks + 1)
    def _(c):
        @pl.when(c < chunks)
        def _():
            alpha_first(c)

        @pl.when(c > 0)
        def _():
            alpha_second(c - 1)

        @pl.when(c < chunks)
        def _():
            add_first(c)

    for c in range(max(0, chunks - 2), chunks):
        wait(rsrecv.at[c], r1_send.at[c])
        wait(ufull.at[0, pl.ds(1, op_size - 1)], g1_send.at[c])

    @loop((chunks - early) * chunks)
    def _(i):
        alpha_piece(early + lax.div(i, chunks), lax.rem(i, chunks))

    q_copy.wait()

    def beta_second(r):
        slot = lax.rem(r, 2)
        at = pl.ds(pl.multiple_of(r * block, block), block)
        wait(wrecv.at[r], w_recv.at[r])
        for c in range(chunks):
            keep(me * chunks + c, ysend[c, 0, at])

        @loop(shards, 1)
        def _(d):
            for c in range(chunks):
                keep(peer(d) * chunks + c, wrecv[r, c, d - 1])

        @pl.when(r >= 2)
        def _():
            wait(rsrecv.at[r - 2], r2_send.at[r - 2])

        group = math.gcd(share, 4)

        @loop(blocks // group)
        def _(i):
            for g in range(group):
                b = i * group + g
                here = pl.ds(pl.multiple_of(lax.rem(b, share) * block, block), block)
                part[slot, mate(lax.div(b, share)), here] = scale * beta(small, b, block)

        for q in range(1, op_size):
            to_mate(
                part.at[slot, q], rsrecv.at[r, q - 1], r2_send.at[r], r2_recv.at[r], q
            )

    def add_second(r):
        slot = lax.rem(r, 2)
        at = pl.ds(pl.multiple_of(r * block, block), block)
        wait(rsrecv.at[r], r2_recv.at[r])
        for j in range(share):
            here, columns = pl.ds(j * block, block), pl.ds(j * block, block)
            total = part[slot, 0, here]
            for q in range(1, op_size):
                total = total + rsrecv[r, q - 1, here]
            vq[at, columns] = total - vq[at, columns]
        pltpu.make_async_copy(vq.at[at], out_hbm.at[at, quarter], o_sem.at[r]).start()
        for q in range(1, op_size):
            to_mate(vq.at[at], out_hbm.at[at, quarter], g2_send, g2_recv, q)

    @loop(chunks + 1)
    def _(r):
        @pl.when(r < chunks)
        def _():
            beta_second(r)

        @pl.when(r > 0)
        def _():
            add_second(r - 1)

    others = pl.ds(0, (op_size - 1) * share * block)
    wait(out_hbm.at[:, others], g2_recv)
    wait(out_hbm.at[:, others], g2_send)
    for r in range(chunks):
        wait(vq.at[pl.ds(r * block, block)], o_sem.at[r])
        wait(wrecv.at[r], w_send.at[r])
    for r in range(max(0, chunks - 2), chunks):
        wait(rsrecv.at[r], r2_send.at[r])


def per_device(coeffs, previous, block_values, block_cols):
    op_size, shards = lax.axis_size("op"), lax.axis_size("str")
    scale = 2.0 / math.sqrt(block_values.shape[0] * op_size)
    values = block_values[0]
    cols = block_cols[0].reshape(-1)
    blocks, slots, block, _ = values.shape
    rows, width = coeffs.shape
    chunks = blocks // shards
    piece = rows // op_size
    segment = width // op_size
    vmem, dma = pltpu.VMEM, pltpu.SemaphoreType.DMA
    anywhere = pl.BlockSpec(memory_space=pl.ANY)
    return pl.pallas_call(
        functools.partial(body, shards, op_size, slots, block, chunks, scale),
        out_shape=jax.ShapeDtypeStruct((rows, width), F32),
        in_specs=[pl.BlockSpec(memory_space=pltpu.SMEM), anywhere, anywhere, anywhere],
        out_specs=anywhere,
        scratch_shapes=[
            vmem((blocks, slots, block, block), BF16),
            vmem((blocks, 2 * rows, block), BF16),
            vmem((chunks, shards, rows + piece, block), F32),
            vmem((chunks, shards - 1, rows + piece, block), F32),
            vmem((chunks, chunks, shards - 1, block, block), F32),
            vmem((blocks, 2 * block, block), BF16),
            vmem((2, op_size, segment, block), F32),
            vmem((2, op_size, segment, block), F32),
            vmem((chunks, op_size - 1, segment, block), F32),
            vmem((2, rows, rows), F32),
            vmem((rows, segment), F32),
            dma, dma((2,)), dma, dma, dma((chunks,)),
            dma((chunks,)), dma((chunks,)), dma((chunks,)),
            dma((chunks,)), dma((chunks,)), dma((chunks,)),
            dma((chunks,)), dma((chunks,)), dma((chunks,)), dma((chunks,)),
            dma, dma,
        ],
        compiler_params=pltpu.CompilerParams(
            collective_id=0, has_side_effects=True, vmem_limit_bytes=VMEM_LIMIT
        ),
        cost_estimate=pl.CostEstimate(
            flops=16 * blocks * slots * block * block * rows,
            bytes_accessed=32 * rows * width,
            transcendentals=0,
        ),
    )(cols, values, coeffs, previous)


def solution(mesh):
    placed = (P("str", None), P("str", None), P("op", None, None, None, None), P("op", None, None))
    return jax.shard_map(
        per_device, mesh=mesh, in_specs=placed, out_specs=P("str", None), check_vma=False
    )
```

```python
import functools
import math

import jax
import jax.numpy as jnp
from jax import lax
from jax.experimental import pallas as pl
from jax.experimental.pallas import tpu as pltpu
from jax.sharding import PartitionSpec as P

F32, BF16 = jnp.float32, jnp.bfloat16
VMEM_LIMIT = 67_043_328


def split(x):
    high = x.astype(BF16)
    return high, (x - high.astype(F32)).astype(BF16)


def flip(a, b, size):
    total, bit = 0, 1
    while bit < size:
        total = total + bit * lax.rem(lax.div(a, bit) + lax.div(b, bit), 2)
        bit *= 2
    return total


def body(
    shards, op_size, slots, block, chunks, scale,
    cols_ref, a_hbm, v_hbm, p_hbm, out_hbm,
    a_ref, field, ysend, yrecv, wrecv, precv, small, part, ufull, rsrecv, vstage, vq,
    a_sem, v_sem, q_sem, o_sem,
    y_send, y_recv, p_send, p_recv, r1_send, r1_recv, g1_send, g1_recv,
    w_send, w_recv, r2_send, r2_recv, g2_send, g2_recv,
):
    blocks = chunks * shards
    rows = chunks * block
    piece = rows // op_size
    thin = min(block, piece)
    wide = rows
    share = blocks // op_size
    segment = share * block
    early = max(1, chunks - 1)
    ahead = min(chunks, max(2, chunks - 2))
    bits = max(1, op_size.bit_length() - 1)
    i32 = jnp.int32
    me, op = lax.axis_index("str").astype(i32), lax.axis_index("op").astype(i32)

    def cuts(n):
        marks = [n * p // bits // 8 * 8 for p in range(bits)] + [n]
        return [(marks[p], marks[p + 1] - marks[p]) for p in range(bits)]

    def first_bit(q, order):
        return next(i for i, b in enumerate(order) if q >> b & 1)

    orders = [[(p + i) % bits for i in range(bits)] for p in range(bits)]
    stages = [
        [
            (p, q, orders[p][i])
            for p in range(bits)
            for q in range(1, op_size)
            if first_bit(q, orders[p]) == i
        ]
        for i in range(bits)
    ]

    def peer(d):
        return flip(me, jnp.asarray(d, i32), shards)

    def mate(q):
        return flip(op, jnp.asarray(q, i32), op_size)

    def wait(ref, sem):
        pltpu.make_async_copy(ref, ref, sem).wait()

    def to_peer(src, dst, send, recv, d):
        pltpu.make_async_remote_copy(
            src_ref=src, dst_ref=dst, send_sem=send, recv_sem=recv,
            device_id={"str": peer(d)}, device_id_type=pl.DeviceIdType.MESH,
        ).start()

    def to_mate(src, dst, send, recv, q):
        pltpu.make_async_remote_copy(
            src_ref=src, dst_ref=dst, send_sem=send, recv_sem=recv,
            device_id={"op": mate(q)}, device_id_type=pl.DeviceIdType.MESH,
        ).start()

    def loop(n, start=0):
        def run(step):
            lax.fori_loop(start, n, lambda i, _: (step(i), None)[1], None)
        return run

    def v_copy(g):
        return pltpu.make_async_copy(
            v_hbm.at[:, pl.ds(pl.multiple_of(g * wide, block), wide)],
            vstage.at[lax.rem(g, 2)],
            v_sem.at[lax.rem(g, 2)],
        )

    def p_part(c, d):
        at = pl.multiple_of((peer(d) * chunks + c) * block, block)
        return p_hbm.at[pl.ds(pl.multiple_of(op * piece, piece), piece), pl.ds(at, block)]

    def send_previous(c, d):
        to_peer(p_part(c, d), precv.at[c, d], p_send.at[c], p_recv.at[c], d)

    a_copy = pltpu.make_async_copy(a_hbm, a_ref, a_sem)
    quarter = pl.ds(pl.multiple_of(op * segment, block), segment)
    q_copy = pltpu.make_async_copy(v_hbm.at[:, quarter], vq, q_sem)

    v_copy(jnp.int32(0)).start()
    a_copy.start()

    barrier = pltpu.get_barrier_semaphore()
    for d in range(1, shards):
        pl.semaphore_signal(
            barrier, inc=1, device_id={"str": peer(d)}, device_id_type=pl.DeviceIdType.MESH
        )
    for q in range(1, op_size):
        pl.semaphore_signal(
            barrier, inc=1, device_id={"op": mate(q)}, device_id_type=pl.DeviceIdType.MESH
        )

    for c in range(chunks):
        pltpu.make_async_copy(p_part(c, 0), precv.at[c, 0], o_sem.at[c]).start()
    pl.semaphore_wait(barrier, shards - 1 + op_size - 1)

    @loop(shards, 1)
    def _(d):
        send_previous(0, d)

    @loop(shards)
    def _(g):
        @pl.when(g + 1 < shards)
        def _():
            v_copy(g + 1).start()

        v_copy(g).wait()
        for i in range(chunks):
            high, low = split(vstage[lax.rem(g, 2), :, i * block : (i + 1) * block])
            field[g * chunks + i, :rows] = high
            field[g * chunks + i, rows:] = low

    a_copy.wait()
    for c in range(chunks):
        wait(precv.at[c, 0], o_sem.at[c])

    def operator_row(row):
        return jnp.concatenate([a_ref[row, j] for j in range(slots)], axis=1)

    def beta(source, row, m):
        left = jnp.concatenate(
            [source[cols_ref[row * slots + j]] for j in range(slots)], axis=1
        )
        both = lax.dot_general(
            left, operator_row(row), (((1,), (1,)), ((), ())), preferred_element_type=F32
        )
        return both[:m] + both[m:]

    def alpha(load, row):
        right = jnp.concatenate(
            [
                jnp.concatenate(load(cols_ref[row * slots + j]), axis=1)
                for j in range(slots)
            ],
            axis=0,
        )
        both = jnp.dot(operator_row(row), right, preferred_element_type=F32)
        return both[:, :block] + both[:, block:]

    def send_stage(slot, c, stage, send, recv):
        for p, q, b in stages[stage]:
            lo, n = cuts(segment)[p]
            to_mate(
                part.at[slot, q, pl.ds(lo, n)], rsrecv.at[c, q - 1, pl.ds(lo, n)],
                send.at[c, q - 1, p], recv.at[c, q - 1, p], 1 << b,
            )

    def arrived(c, stage, recv):
        for p, q, b in stages[stage]:
            lo, n = cuts(segment)[p]
            wait(rsrecv.at[c, q - 1, pl.ds(lo, n)], recv.at[c, q - 1, p])

    def relay_stages(slot, c, send, recv):
        for stage in range(bits - 1):
            arrived(c, stage, recv)
            for p, q, b in stages[stage]:
                left = q ^ (1 << b)
                if left:
                    lo, n = cuts(segment)[p]
                    here = pl.ds(lo, n)
                    part[slot, left, here] = part[slot, left, here] + rsrecv[c, q - 1, here]
            send_stage(slot, c, stage + 1, send, recv)

    def sum_sent(c, send):
        for p in range(bits):
            lo, n = cuts(segment)[p]
            for q in range(1, op_size):
                wait(rsrecv.at[c, q - 1, pl.ds(lo, n)], send.at[c, q - 1, p])

    def own_total(slot, c, at, n):
        here = pl.ds(at, n)
        total = part[slot, 0, here]
        for b in range(bits):
            total = total + rsrecv[c, (1 << b) - 1, here]
        return total

    def hand_out(c, copy, have):
        for p in range(bits):
            order = orders[p][::-1]
            for q in range(1, op_size):
                last = max(i for i, b in enumerate(order) if q >> b & 1)
                source = q ^ (1 << order[last])
                if source in have:
                    copy(c, p, source, q, 1 << order[last])

    waves = [[q for q in range(op_size) if bin(q).count("1") == n] for n in range(bits + 1)]

    def beta_first(c):
        @loop(shards)
        def _(d):
            ysend[c, d] = beta(field, peer(d) * chunks + c, rows)

            @pl.when(d > 0)
            def _():
                to_peer(ysend.at[c, d], yrecv.at[c, d - 1], y_send.at[c], y_recv.at[c], d)

                @pl.when(c + 1 < chunks)
                def _():
                    send_previous(c + 1, d)

    def keep(at_block, x):
        high, low = split(x)
        small[at_block, :block] = high
        small[at_block, block:] = low

    def pieces(h):
        for t in range(block // thin):
            g = h * block + t * thin
            yield g // piece, g % piece, t * thin

    def alpha_first(c):
        slot = lax.rem(c, 2)
        wait(yrecv.at[c], y_recv.at[c])
        for h in range(chunks):
            keep(me * chunks + h, ysend[c, 0, h * block : (h + 1) * block])

        @loop(shards, 1)
        def _(d):
            for h in range(chunks):
                keep(peer(d) * chunks + h, yrecv[c, d - 1, h * block : (h + 1) * block])

        @pl.when(c >= 2)
        def _():
            sum_sent(c - 2, r1_send)
            handed_first(c - 2, g1_send, range(1, op_size))

        @loop(shards)
        def _(d):
            for h in range(chunks):
                value = scale * alpha(
                    lambda b: [small[b, :block], small[b, block:]], peer(d) * chunks + h
                )
                for owner, at, start in pieces(h):
                    here = pl.ds(pl.multiple_of(d * piece + at, thin), thin)
                    part[slot, mate(owner), here] = value[start : start + thin]

        send_stage(slot, c, 0, r1_send, r1_recv)

    def hand_first(c, p, source, q, across):
        slot = lax.rem(c, 2)
        lo, n = cuts(segment)[p]
        to_mate(
            ufull.at[slot, source, pl.ds(lo, n)], ufull.at[slot, q, pl.ds(lo, n)],
            g1_send.at[c, q - 1, p], g1_recv.at[c, q - 1, p], across,
        )

    def handed_first(c, sem, slots_):
        for p in range(bits):
            lo, n = cuts(segment)[p]
            for q in slots_:
                wait(ufull.at[lax.rem(c, 2), q, pl.ds(lo, n)], sem.at[c, q - 1, p])

    def add_first(c):
        slot = lax.rem(c, 2)
        relay_stages(slot, c, r1_send, r1_recv)

        @pl.when(c == 0)
        def _():
            q_copy.start()

        wait(precv.at[c, pl.ds(1, shards - 1)], p_recv.at[c])
        arrived(c, bits - 1, r1_recv)

        @loop(shards)
        def _(d):
            at = pl.multiple_of(d * piece, piece)
            ufull[slot, 0, pl.ds(at, piece)] = own_total(slot, c, at, piece) - precv[c, d]

        hand_out(c, hand_first, waves[0])

    def alpha_piece(r, c):
        at = pl.multiple_of(r * block, block)
        column = pl.multiple_of(2 * block * c, 2 * block)

        @loop(shards)
        def _(d):
            ysend[c, d, pl.ds(at, block)] = alpha(
                lambda b: [
                    field[b, pl.ds(column, block)],
                    field[b, pl.ds(column + block, block)],
                ],
                peer(d) * chunks + r,
            )

            @pl.when(d > 0)
            def _():
                to_peer(
                    ysend.at[c, d, pl.ds(at, block)], wrecv.at[r, c, d - 1],
                    w_send.at[r], w_recv.at[r], d,
                )

    def alpha_second(c):
        slot = lax.rem(c, 2)
        for wave in waves[1:]:
            handed_first(c, g1_recv, wave)
            hand_out(c, hand_first, wave)
        column = pl.multiple_of(2 * block * c, 2 * block)

        @loop(shards)
        def _(d):
            for h in range(chunks):
                x = jnp.concatenate(
                    [
                        ufull[slot, mate(owner), pl.ds(pl.multiple_of(d * piece + at, thin), thin)]
                        for owner, at, _ in pieces(h)
                    ],
                    axis=0,
                )
                high, low = split(x)
                field[peer(d) * chunks + h, pl.ds(column, block)] = high
                field[peer(d) * chunks + h, pl.ds(column + block, block)] = low

        wait(yrecv.at[c], y_send.at[c])

        @loop(early)
        def _(r):
            alpha_piece(r, c)

    @loop(ahead)
    def _(c):
        beta_first(c)

    @loop(chunks + 1)
    def _(c):
        @pl.when(c < chunks)
        def _():
            alpha_first(c)

        @pl.when(c + ahead < chunks)
        def _():
            beta_first(c + ahead)

        @pl.when(c > 0)
        def _():
            alpha_second(c - 1)

        @pl.when(c < chunks)
        def _():
            add_first(c)

    @loop((chunks - early) * chunks)
    def _(i):
        alpha_piece(early + lax.div(i, chunks), lax.rem(i, chunks))

    for c in range(max(0, chunks - 2), chunks):
        sum_sent(c, r1_send)
        handed_first(c, g1_send, range(1, op_size))
    q_copy.wait()

    def row_block(r):
        return pl.ds(pl.multiple_of(r * block, block), block)

    def beta_second(r):
        slot = lax.rem(r, 2)
        at = row_block(r)
        wait(wrecv.at[r], w_recv.at[r])
        for c in range(chunks):
            keep(me * chunks + c, ysend[c, 0, at])

        @loop(shards, 1)
        def _(d):
            for c in range(chunks):
                keep(peer(d) * chunks + c, wrecv[r, c, d - 1])

        @pl.when(r >= 2)
        def _():
            sum_sent(r - 2, r2_send)

        group = math.gcd(share, 4)

        @loop(blocks // group)
        def _(i):
            for g in range(group):
                b = i * group + g
                here = pl.ds(pl.multiple_of(lax.rem(b, share) * block, block), block)
                part[slot, mate(lax.div(b, share)), here] = scale * beta(small, b, block)

        send_stage(slot, r, 0, r2_send, r2_recv)

    def out_part(r, p, q):
        lo, n = cuts(block)[p]
        here = pl.ds(pl.multiple_of(r * block + lo, 8), n)
        return out_hbm.at[here, pl.ds(pl.multiple_of(mate(q) * segment, segment), segment)]

    def hand_second(r, p, source, q, across):
        lo, n = cuts(block)[p]
        own = vq.at[pl.ds(pl.multiple_of(r * block + lo, 8), n)]
        there = out_part(r, p, source)
        to_mate(
            there if source else own, there,
            g2_send.at[r, q - 1, p], g2_recv.at[r, q - 1, p], across,
        )

    def add_second(r):
        slot = lax.rem(r, 2)
        at = row_block(r)
        arrived(r, bits - 1, r2_recv)
        for j in range(share):
            columns = pl.ds(j * block, block)
            vq[at, columns] = own_total(slot, r, j * block, block) - vq[at, columns]
        hand_out(r, hand_second, waves[0])
        pltpu.make_async_copy(vq.at[at], out_hbm.at[at, quarter], o_sem.at[r]).start()

    def handed_second(r, sem, slots_):
        for p in range(bits):
            for q in slots_:
                wait(out_part(r, p, q), sem.at[r, q - 1, p])

    def relay_second(r):
        for wave in waves[1:]:
            handed_second(r, g2_recv, wave)
            hand_out(r, hand_second, wave)

    def at_tick(t, act):
        last = chunks + 1
        early_one = jnp.logical_and(t >= 0, t < chunks - 1)

        @pl.when(jnp.logical_or(early_one, t == last))
        def _():
            act(jnp.minimum(t, chunks - 1))

    @loop(chunks + 5)
    def _(t):
        at_tick(t - 3, relay_second)
        at_tick(t - 2, add_second)
        at_tick(t, beta_second)
        at_tick(t - 1, lambda r: relay_stages(lax.rem(r, 2), r, r2_send, r2_recv))

    for r in range(chunks):
        handed_second(r, g2_send, range(1, op_size))
        wait(vq.at[pl.ds(r * block, block)], o_sem.at[r])
        wait(wrecv.at[r], w_send.at[r])
        wait(precv.at[r, pl.ds(1, shards - 1)], p_send.at[r])
    for r in range(max(0, chunks - 2), chunks):
        sum_sent(r, r2_send)


def per_device(coeffs, previous, block_values, block_cols):
    op_size, shards = lax.axis_size("op"), lax.axis_size("str")
    scale = 2.0 / math.sqrt(block_values.shape[0] * op_size)
    values = block_values[0]
    cols = block_cols[0].reshape(-1)
    blocks, slots, block, _ = values.shape
    rows, width = coeffs.shape
    chunks = blocks // shards
    piece = rows // op_size
    segment = width // op_size
    paths = (chunks, op_size - 1, max(1, op_size.bit_length() - 1))
    vmem, dma = pltpu.VMEM, pltpu.SemaphoreType.DMA
    anywhere = pl.BlockSpec(memory_space=pl.ANY)
    return pl.pallas_call(
        functools.partial(body, shards, op_size, slots, block, chunks, scale),
        out_shape=jax.ShapeDtypeStruct((rows, width), F32),
        in_specs=[pl.BlockSpec(memory_space=pltpu.SMEM), anywhere, anywhere, anywhere],
        out_specs=anywhere,
        scratch_shapes=[
            vmem((blocks, slots, block, block), BF16),
            vmem((blocks, 2 * rows, block), BF16),
            vmem((chunks, shards, rows, block), F32),
            vmem((chunks, shards - 1, rows, block), F32),
            vmem((chunks, chunks, shards - 1, block, block), F32),
            vmem((chunks, shards, piece, block), F32),
            vmem((blocks, 2 * block, block), BF16),
            vmem((2, op_size, segment, block), F32),
            vmem((2, op_size, segment, block), F32),
            vmem((chunks, op_size - 1, segment, block), F32),
            vmem((2, rows, rows), F32),
            vmem((rows, segment), F32),
            dma, dma((2,)), dma, dma((chunks,)),
            dma((chunks,)), dma((chunks,)), dma((chunks,)), dma((chunks,)),
            dma(paths), dma(paths), dma(paths), dma(paths),
            dma((chunks,)), dma((chunks,)),
            dma(paths), dma(paths), dma(paths), dma(paths),
        ],
        compiler_params=pltpu.CompilerParams(
            collective_id=0, has_side_effects=True, vmem_limit_bytes=VMEM_LIMIT
        ),
        cost_estimate=pl.CostEstimate(
            flops=16 * blocks * slots * block * block * rows,
            bytes_accessed=32 * rows * width,
            transcendentals=0,
        ),
    )(cols, values, coeffs, previous)


def solution(mesh):
    placed = (P("str", None), P("str", None), P("op", None, None, None, None), P("op", None, None))
    return jax.shard_map(
        per_device, mesh=mesh, in_specs=placed, out_specs=P("str", None), check_vma=False
    )
```

```python
import functools
import math

import jax
import jax.numpy as jnp
from jax import lax
from jax.experimental import pallas as pl
from jax.experimental.pallas import tpu as pltpu
from jax.sharding import PartitionSpec as P

F32, BF16 = jnp.float32, jnp.bfloat16
VMEM_LIMIT = 67_043_328


def split(x):
    high = x.astype(BF16)
    return high, (x - high.astype(F32)).astype(BF16)


def flip(a, b, size):
    total, bit = 0, 1
    while bit < size:
        total = total + bit * lax.rem(lax.div(a, bit) + lax.div(b, bit), 2)
        bit *= 2
    return total


def body(
    shards, op_size, slots, block, chunks, scale,
    cols_ref, a_hbm, v_hbm, p_hbm, out_hbm,
    a_ref, field, ysend, yrecv, wrecv, precv, small, part, ufull, rsrecv, vstage, vq,
    a_sem, v_sem, q_sem, o_sem,
    y_send, y_recv, p_send, p_recv, r1_send, r1_recv, g1_send, g1_recv,
    w_send, w_recv, r2_send, r2_recv, g2_send, g2_recv,
):
    blocks = chunks * shards
    rows = chunks * block
    piece = rows // op_size
    thin = min(block, piece)
    wide = rows
    share = blocks // op_size
    segment = share * block
    early = max(1, chunks // 2)
    near = max(1, shards // 2)
    bits = max(1, op_size.bit_length() - 1)
    i32 = jnp.int32
    me, op = lax.axis_index("str").astype(i32), lax.axis_index("op").astype(i32)

    def cuts(n):
        marks = [n * p // bits // 8 * 8 for p in range(bits)] + [n]
        return [(marks[p], marks[p + 1] - marks[p]) for p in range(bits)]

    def first_bit(q, order):
        return next(i for i, b in enumerate(order) if q >> b & 1)

    orders = [[(p + i) % bits for i in range(bits)] for p in range(bits)]
    stages = [
        [
            (p, q, orders[p][i])
            for p in range(bits)
            for q in range(1, op_size)
            if first_bit(q, orders[p]) == i
        ]
        for i in range(bits)
    ]

    def peer(d):
        return flip(me, jnp.asarray(d, i32), shards)

    def mate(q):
        return flip(op, jnp.asarray(q, i32), op_size)

    def wait(ref, sem):
        pltpu.make_async_copy(ref, ref, sem).wait()

    def to_peer(src, dst, send, recv, d):
        pltpu.make_async_remote_copy(
            src_ref=src, dst_ref=dst, send_sem=send, recv_sem=recv,
            device_id={"str": peer(d)}, device_id_type=pl.DeviceIdType.MESH,
        ).start()

    def to_mate(src, dst, send, recv, q):
        pltpu.make_async_remote_copy(
            src_ref=src, dst_ref=dst, send_sem=send, recv_sem=recv,
            device_id={"op": mate(q)}, device_id_type=pl.DeviceIdType.MESH,
        ).start()

    def loop(n, start=0):
        def run(step):
            lax.fori_loop(start, n, lambda i, _: (step(i), None)[1], None)
        return run

    def v_copy(g):
        return pltpu.make_async_copy(
            v_hbm.at[:, pl.ds(pl.multiple_of(g * wide, block), wide)],
            vstage.at[lax.rem(g, 2)],
            v_sem.at[lax.rem(g, 2)],
        )

    def p_part(c, d):
        at = pl.multiple_of((peer(d) * chunks + c) * block, block)
        return p_hbm.at[pl.ds(pl.multiple_of(op * piece, piece), piece), pl.ds(at, block)]

    def send_previous(c, d):
        to_peer(p_part(c, d), precv.at[c, d], p_send.at[c], p_recv.at[c], d)

    a_copy = pltpu.make_async_copy(a_hbm, a_ref, a_sem)
    quarter = pl.ds(pl.multiple_of(op * segment, block), segment)
    q_copy = pltpu.make_async_copy(v_hbm.at[:, quarter], vq, q_sem)

    v_copy(jnp.int32(0)).start()
    a_copy.start()

    barrier = pltpu.get_barrier_semaphore()
    for d in range(1, shards):
        pl.semaphore_signal(
            barrier, inc=1, device_id={"str": peer(d)}, device_id_type=pl.DeviceIdType.MESH
        )
    for q in range(1, op_size):
        pl.semaphore_signal(
            barrier, inc=1, device_id={"op": mate(q)}, device_id_type=pl.DeviceIdType.MESH
        )

    for c in range(chunks):
        pltpu.make_async_copy(p_part(c, 0), precv.at[c, 0], o_sem.at[c]).start()
    pl.semaphore_wait(barrier, shards - 1 + op_size - 1)

    @loop(shards, 1)
    def _(d):
        send_previous(0, d)

    @loop(shards)
    def _(g):
        @pl.when(g + 1 < shards)
        def _():
            v_copy(g + 1).start()

        v_copy(g).wait()
        for i in range(chunks):
            high, low = split(vstage[lax.rem(g, 2), :, i * block : (i + 1) * block])
            field[g * chunks + i, :rows] = high
            field[g * chunks + i, rows:] = low

    a_copy.wait()
    for c in range(chunks):
        wait(precv.at[c, 0], o_sem.at[c])

    def operator_row(row):
        return jnp.concatenate([a_ref[row, j] for j in range(slots)], axis=1)

    def beta(source, row, m):
        left = jnp.concatenate(
            [source[cols_ref[row * slots + j]] for j in range(slots)], axis=1
        )
        both = lax.dot_general(
            left, operator_row(row), (((1,), (1,)), ((), ())), preferred_element_type=F32
        )
        return both[:m] + both[m:]

    def alpha(load, row):
        right = jnp.concatenate(
            [
                jnp.concatenate(load(cols_ref[row * slots + j]), axis=1)
                for j in range(slots)
            ],
            axis=0,
        )
        both = jnp.dot(operator_row(row), right, preferred_element_type=F32)
        return both[:, :block] + both[:, block:]

    def send_stage(slot, c, stage, send, recv):
        for p, q, b in stages[stage]:
            lo, n = cuts(segment)[p]
            to_mate(
                part.at[slot, q, pl.ds(lo, n)], rsrecv.at[slot, q - 1, pl.ds(lo, n)],
                send.at[c, q - 1, p], recv.at[c, q - 1, p], 1 << b,
            )

    def arrived(slot, c, stage, recv):
        for p, q, b in stages[stage]:
            lo, n = cuts(segment)[p]
            wait(rsrecv.at[slot, q - 1, pl.ds(lo, n)], recv.at[c, q - 1, p])

    def relay_stages(slot, c, send, recv):
        for stage in range(bits - 1):
            arrived(slot, c, stage, recv)
            for p, q, b in stages[stage]:
                left = q ^ (1 << b)
                if left:
                    lo, n = cuts(segment)[p]
                    here = pl.ds(lo, n)
                    part[slot, left, here] = part[slot, left, here] + rsrecv[slot, q - 1, here]
            send_stage(slot, c, stage + 1, send, recv)

    def sum_sent(c, send):
        for p in range(bits):
            lo, n = cuts(segment)[p]
            for q in range(1, op_size):
                wait(rsrecv.at[0, q - 1, pl.ds(lo, n)], send.at[c, q - 1, p])

    def own_total(slot, at, n):
        here = pl.ds(at, n)
        total = part[slot, 0, here]
        for b in range(bits):
            total = total + rsrecv[slot, (1 << b) - 1, here]
        return total

    def hand_out(c, copy, have):
        for p in range(bits):
            order = orders[p][::-1]
            for q in range(1, op_size):
                last = max(i for i, b in enumerate(order) if q >> b & 1)
                source = q ^ (1 << order[last])
                if source in have:
                    copy(c, p, source, q, 1 << order[last])

    waves = [[q for q in range(op_size) if bin(q).count("1") == n] for n in range(bits + 1)]

    def beta_first(c, start, end):
        @loop(end, start)
        def _(d):
            ysend[c, d] = beta(field, peer(d) * chunks + c, rows)

            @pl.when(d > 0)
            def _():
                to_peer(ysend.at[c, d], yrecv.at[c, d - 1], y_send.at[c], y_recv.at[c], d)

                @pl.when(c + 1 < chunks)
                def _():
                    send_previous(c + 1, d)

    def keep(at_block, x):
        high, low = split(x)
        small[at_block, :block] = high
        small[at_block, block:] = low

    def pieces(h):
        for t in range(block // thin):
            g = h * block + t * thin
            yield g // piece, g % piece, t * thin

    def alpha_first(c):
        slot = lax.rem(c, 2)
        for h in range(chunks):
            keep(me * chunks + h, ysend[c, 0, h * block : (h + 1) * block])

        @loop(shards, 1)
        def _(d):
            for h in range(chunks):
                keep(peer(d) * chunks + h, yrecv[c, d - 1, h * block : (h + 1) * block])

        @pl.when(c >= 2)
        def _():
            sum_sent(c - 2, r1_send)

        @loop(shards)
        def _(d):
            for h in range(chunks):
                value = scale * alpha(
                    lambda b: [small[b, :block], small[b, block:]], peer(d) * chunks + h
                )
                for owner, at, start in pieces(h):
                    here = pl.ds(pl.multiple_of(d * piece + at, thin), thin)
                    part[slot, mate(owner), here] = value[start : start + thin]

        send_stage(slot, c, 0, r1_send, r1_recv)

    def hand_first(c, p, source, q, across):
        lo, n = cuts(segment)[p]
        to_mate(
            ufull.at[c, source, pl.ds(lo, n)], ufull.at[c, q, pl.ds(lo, n)],
            g1_send.at[c, q - 1, p], g1_recv.at[c, q - 1, p], across,
        )

    def handed_first(c, sem, slots_):
        for p in range(bits):
            lo, n = cuts(segment)[p]
            for q in slots_:
                wait(ufull.at[c, q, pl.ds(lo, n)], sem.at[c, q - 1, p])

    def add_first(c):
        slot = lax.rem(c, 2)
        relay_stages(slot, c, r1_send, r1_recv)

        @pl.when(c == 0)
        def _():
            q_copy.start()

        wait(precv.at[c, pl.ds(1, shards - 1)], p_recv.at[c])
        arrived(slot, c, bits - 1, r1_recv)

        @loop(shards)
        def _(d):
            at = pl.multiple_of(d * piece, piece)
            ufull[c, 0, pl.ds(at, piece)] = own_total(slot, at, piece) - precv[c, d]

        hand_out(c, hand_first, waves[0])

    def alpha_piece(r, c):
        at = pl.multiple_of(r * block, block)
        column = pl.multiple_of(2 * block * c, 2 * block)

        @loop(shards)
        def _(d):
            ysend[c, d, pl.ds(at, block)] = alpha(
                lambda b: [
                    field[b, pl.ds(column, block)],
                    field[b, pl.ds(column + block, block)],
                ],
                peer(d) * chunks + r,
            )

            @pl.when(d > 0)
            def _():
                to_peer(
                    ysend.at[c, d, pl.ds(at, block)], wrecv.at[r, c, d - 1],
                    w_send.at[r], w_recv.at[r], d,
                )

    def relay_first(c):
        for wave in waves[1:-1]:
            handed_first(c, g1_recv, wave)
            hand_out(c, hand_first, wave)

    def alpha_second(c):
        handed_first(c, g1_recv, waves[-1])
        column = pl.multiple_of(2 * block * c, 2 * block)

        @loop(shards)
        def _(d):
            for h in range(chunks):
                x = jnp.concatenate(
                    [
                        ufull[c, mate(owner), pl.ds(pl.multiple_of(d * piece + at, thin), thin)]
                        for owner, at, _ in pieces(h)
                    ],
                    axis=0,
                )
                high, low = split(x)
                field[peer(d) * chunks + h, pl.ds(column, block)] = high
                field[peer(d) * chunks + h, pl.ds(column + block, block)] = low

        wait(yrecv.at[c], y_send.at[c])

        @loop(early)
        def _(r):
            alpha_piece(r, c)

    beta_first(0, 0, shards)
    if chunks > 1:
        beta_first(1, 0, near)

    @loop(chunks)
    def _(c):
        wait(yrecv.at[c], y_recv.at[c])

        @pl.when(c + 1 < chunks)
        def _():
            beta_first(c + 1, near, shards)

        @pl.when(c + 2 < chunks)
        def _():
            beta_first(c + 2, 0, near)

        alpha_first(c)

        @pl.when(c == chunks - 1)
        def _():
            loop(chunks - 1)(alpha_second)

        add_first(c)
        relay_first(c)

    alpha_second(chunks - 1)

    @loop((chunks - early) * chunks)
    def _(i):
        alpha_piece(early + lax.div(i, chunks), lax.rem(i, chunks))

    for c in range(max(0, chunks - 2), chunks):
        sum_sent(c, r1_send)
    for c in range(chunks):
        handed_first(c, g1_send, range(1, op_size))
    q_copy.wait()

    def row_block(r):
        return pl.ds(pl.multiple_of(r * block, block), block)

    def beta_second(r):
        slot = lax.rem(r, 2)
        at = row_block(r)
        wait(wrecv.at[r], w_recv.at[r])
        for c in range(chunks):
            keep(me * chunks + c, ysend[c, 0, at])

        @loop(shards, 1)
        def _(d):
            for c in range(chunks):
                keep(peer(d) * chunks + c, wrecv[r, c, d - 1])

        @pl.when(r >= 2)
        def _():
            sum_sent(r - 2, r2_send)

        group = math.gcd(share, 4)

        @loop(blocks // group)
        def _(i):
            for g in range(group):
                b = i * group + g
                here = pl.ds(pl.multiple_of(lax.rem(b, share) * block, block), block)
                part[slot, mate(lax.div(b, share)), here] = scale * beta(small, b, block)

        send_stage(slot, r, 0, r2_send, r2_recv)

    def out_part(r, p, q):
        lo, n = cuts(block)[p]
        here = pl.ds(pl.multiple_of(r * block + lo, 8), n)
        return out_hbm.at[here, pl.ds(pl.multiple_of(mate(q) * segment, segment), segment)]

    def hand_second(r, p, source, q, across):
        lo, n = cuts(block)[p]
        own = vq.at[pl.ds(pl.multiple_of(r * block + lo, 8), n)]
        there = out_part(r, p, source)
        to_mate(
            there if source else own, there,
            g2_send.at[r, q - 1, p], g2_recv.at[r, q - 1, p], across,
        )

    def add_second(r):
        slot = lax.rem(r, 2)
        at = row_block(r)
        arrived(slot, r, bits - 1, r2_recv)
        for j in range(share):
            columns = pl.ds(j * block, block)
            vq[at, columns] = own_total(slot, j * block, block) - vq[at, columns]
        hand_out(r, hand_second, waves[0])
        pltpu.make_async_copy(vq.at[at], out_hbm.at[at, quarter], o_sem.at[r]).start()

    def handed_second(r, sem, slots_):
        for p in range(bits):
            for q in slots_:
                wait(out_part(r, p, q), sem.at[r, q - 1, p])

    def relay_second(r):
        for wave in waves[1:]:
            handed_second(r, g2_recv, wave)
            hand_out(r, hand_second, wave)

    acts = {
        "beta": beta_second,
        "relay": lambda r: relay_stages(lax.rem(r, 2), r, r2_send, r2_recv),
        "add": add_second,
        "hand": relay_second,
    }
    pair = range(min(2, chunks))
    order = [(act, r) for act in ("beta", "relay", "add", "hand") for r in pair]
    for r in range(2, chunks):
        at = len(order) - 1 if r == 2 else len(order)
        order.insert(at, ("beta", r))
        order += [(act, r) for act in ("relay", "add", "hand")]

    @loop(len(order))
    def _(t):
        for name, act in acts.items():
            ticks = [order.index((name, r)) for r in range(chunks)]
            now = functools.reduce(jnp.logical_or, [t == k for k in ticks])
            r = sum(jnp.minimum(jnp.maximum(t - k + 1, 0), 1) for k in ticks) - 1

            @pl.when(now)
            def _():
                act(r)

    for r in range(chunks):
        handed_second(r, g2_send, range(1, op_size))
        wait(vq.at[pl.ds(r * block, block)], o_sem.at[r])
        wait(wrecv.at[r], w_send.at[r])
        wait(precv.at[r, pl.ds(1, shards - 1)], p_send.at[r])
    for r in range(max(0, chunks - 2), chunks):
        sum_sent(r, r2_send)


def per_device(coeffs, previous, block_values, block_cols):
    op_size, shards = lax.axis_size("op"), lax.axis_size("str")
    scale = 2.0 / math.sqrt(block_values.shape[0] * op_size)
    values = block_values[0]
    cols = block_cols[0].reshape(-1)
    blocks, slots, block, _ = values.shape
    rows, width = coeffs.shape
    chunks = blocks // shards
    piece = rows // op_size
    segment = width // op_size
    paths = (chunks, op_size - 1, max(1, op_size.bit_length() - 1))
    vmem, dma = pltpu.VMEM, pltpu.SemaphoreType.DMA
    anywhere = pl.BlockSpec(memory_space=pl.ANY)
    return pl.pallas_call(
        functools.partial(body, shards, op_size, slots, block, chunks, scale),
        out_shape=jax.ShapeDtypeStruct((rows, width), F32),
        in_specs=[pl.BlockSpec(memory_space=pltpu.SMEM), anywhere, anywhere, anywhere],
        out_specs=anywhere,
        scratch_shapes=[
            vmem((blocks, slots, block, block), BF16),
            vmem((blocks, 2 * rows, block), BF16),
            vmem((chunks, shards, rows, block), F32),
            vmem((chunks, shards - 1, rows, block), F32),
            vmem((chunks, chunks, shards - 1, block, block), F32),
            vmem((chunks, shards, piece, block), F32),
            vmem((blocks, 2 * block, block), BF16),
            vmem((2, op_size, segment, block), F32),
            vmem((chunks, op_size, segment, block), F32),
            vmem((2, op_size - 1, segment, block), F32),
            vmem((2, rows, rows), F32),
            vmem((rows, segment), F32),
            dma, dma((2,)), dma, dma((chunks,)),
            dma((chunks,)), dma((chunks,)), dma((chunks,)), dma((chunks,)),
            dma(paths), dma(paths), dma(paths), dma(paths),
            dma((chunks,)), dma((chunks,)),
            dma(paths), dma(paths), dma(paths), dma(paths),
        ],
        compiler_params=pltpu.CompilerParams(
            collective_id=0, has_side_effects=True, vmem_limit_bytes=VMEM_LIMIT
        ),
        cost_estimate=pl.CostEstimate(
            flops=16 * blocks * slots * block * block * rows,
            bytes_accessed=32 * rows * width,
            transcendentals=0,
        ),
    )(cols, values, coeffs, previous)


def solution(mesh):
    placed = (P("str", None), P("str", None), P("op", None, None, None, None), P("op", None, None))
    return jax.shard_map(
        per_device, mesh=mesh, in_specs=placed, out_specs=P("str", None), check_vma=False
    )
```

```python
import functools
import math

import jax
import jax.numpy as jnp
from jax import lax
from jax.experimental import pallas as pl
from jax.experimental.pallas import tpu as pltpu
from jax.sharding import PartitionSpec as P

F32, BF16 = jnp.float32, jnp.bfloat16
VMEM_LIMIT = 67_043_328


def split(x):
    high = x.astype(BF16)
    return high, (x - high.astype(F32)).astype(BF16)


def flip(a, b, size):
    total, bit = 0, 1
    while bit < size:
        total = total + bit * lax.rem(lax.div(a, bit) + lax.div(b, bit), 2)
        bit *= 2
    return total


def body(
    shards, op_size, slots, block, chunks, scale,
    cols_ref, a_hbm, v_hbm, p_hbm, out_hbm,
    a_ref, field, ysend, yrecv, wrecv, precv, small, part, ufull, rsrecv, vstage, vq,
    a_sem, v_sem, q_sem, o_sem,
    y_send, y_recv, p_send, p_recv, r1_send, r1_recv, g1_send, g1_recv,
    w_send, w_recv, r2_send, r2_recv, g2_send, g2_recv,
):
    blocks = chunks * shards
    rows = chunks * block
    piece = rows // op_size
    thin = min(block, piece)
    wide = rows
    share = blocks // op_size
    segment = share * block
    early = max(1, chunks // 2)
    near = max(1, shards // 2)
    bits = max(1, op_size.bit_length() - 1)
    i32 = jnp.int32
    me, op = lax.axis_index("str").astype(i32), lax.axis_index("op").astype(i32)

    def cuts(n):
        marks = [n * p // bits // 8 * 8 for p in range(bits)] + [n]
        return [(marks[p], marks[p + 1] - marks[p]) for p in range(bits)]

    def first_bit(q, order):
        return next(i for i, b in enumerate(order) if q >> b & 1)

    orders = [[(p + i) % bits for i in range(bits)] for p in range(bits)]
    stages = [
        [
            (p, q, orders[p][i])
            for p in range(bits)
            for q in range(1, op_size)
            if first_bit(q, orders[p]) == i
        ]
        for i in range(bits)
    ]

    def peer(d):
        return flip(me, jnp.asarray(d, i32), shards)

    def mate(q):
        return flip(op, jnp.asarray(q, i32), op_size)

    def wait(ref, sem):
        pltpu.make_async_copy(ref, ref, sem).wait()

    def to_peer(src, dst, send, recv, d):
        pltpu.make_async_remote_copy(
            src_ref=src, dst_ref=dst, send_sem=send, recv_sem=recv,
            device_id={"str": peer(d)}, device_id_type=pl.DeviceIdType.MESH,
        ).start()

    def to_mate(src, dst, send, recv, q):
        pltpu.make_async_remote_copy(
            src_ref=src, dst_ref=dst, send_sem=send, recv_sem=recv,
            device_id={"op": mate(q)}, device_id_type=pl.DeviceIdType.MESH,
        ).start()

    def loop(n, start=0):
        def run(step):
            lax.fori_loop(start, n, lambda i, _: (step(i), None)[1], None)
        return run

    def v_copy(g):
        return pltpu.make_async_copy(
            v_hbm.at[:, pl.ds(pl.multiple_of(g * wide, block), wide)],
            vstage.at[lax.rem(g, 2)],
            v_sem.at[lax.rem(g, 2)],
        )

    def p_part(c, d):
        at = pl.multiple_of((peer(d) * chunks + c) * block, block)
        return p_hbm.at[pl.ds(pl.multiple_of(op * piece, piece), piece), pl.ds(at, block)]

    def send_previous(c, d):
        to_peer(p_part(c, d), precv.at[c, d], p_send.at[c], p_recv.at[c], d)

    a_copy = pltpu.make_async_copy(a_hbm, a_ref, a_sem)
    quarter = pl.ds(pl.multiple_of(op * segment, block), segment)
    q_copy = pltpu.make_async_copy(v_hbm.at[:, quarter], vq, q_sem)

    v_copy(jnp.int32(0)).start()
    a_copy.start()

    barrier = pltpu.get_barrier_semaphore()
    for d in range(1, shards):
        pl.semaphore_signal(
            barrier, inc=1, device_id={"str": peer(d)}, device_id_type=pl.DeviceIdType.MESH
        )
    for q in range(1, op_size):
        pl.semaphore_signal(
            barrier, inc=1, device_id={"op": mate(q)}, device_id_type=pl.DeviceIdType.MESH
        )

    for c in range(chunks):
        pltpu.make_async_copy(p_part(c, 0), precv.at[c, 0], o_sem.at[c]).start()
    pl.semaphore_wait(barrier, shards - 1 + op_size - 1)

    @loop(shards, 1)
    def _(d):
        send_previous(0, d)

    @loop(shards)
    def _(g):
        @pl.when(g + 1 < shards)
        def _():
            v_copy(g + 1).start()

        v_copy(g).wait()
        for i in range(chunks):
            high, low = split(vstage[lax.rem(g, 2), :, i * block : (i + 1) * block])
            field[g * chunks + i, :rows] = high
            field[g * chunks + i, rows:] = low

    a_copy.wait()
    for c in range(chunks):
        wait(precv.at[c, 0], o_sem.at[c])

    def operator_row(row):
        return jnp.concatenate([a_ref[row, j] for j in range(slots)], axis=1)

    def beta(source, row, m):
        left = jnp.concatenate(
            [source[cols_ref[row * slots + j]] for j in range(slots)], axis=1
        )
        both = lax.dot_general(
            left, operator_row(row), (((1,), (1,)), ((), ())), preferred_element_type=F32
        )
        return both[:m] + both[m:]

    def alpha(load, row):
        right = jnp.concatenate(
            [
                jnp.concatenate(load(cols_ref[row * slots + j]), axis=1)
                for j in range(slots)
            ],
            axis=0,
        )
        both = jnp.dot(operator_row(row), right, preferred_element_type=F32)
        return both[:, :block] + both[:, block:]

    def send_stage(slot, c, stage, send, recv):
        for p, q, b in stages[stage]:
            lo, n = cuts(segment)[p]
            to_mate(
                part.at[slot, q, pl.ds(lo, n)], rsrecv.at[slot, q - 1, pl.ds(lo, n)],
                send.at[c, q - 1, p], recv.at[c, q - 1, p], 1 << b,
            )

    def arrived(slot, c, stage, recv):
        for p, q, b in stages[stage]:
            lo, n = cuts(segment)[p]
            wait(rsrecv.at[slot, q - 1, pl.ds(lo, n)], recv.at[c, q - 1, p])

    def relay_stages(slot, c, send, recv):
        for stage in range(bits - 1):
            arrived(slot, c, stage, recv)
            for p, q, b in stages[stage]:
                left = q ^ (1 << b)
                if left:
                    lo, n = cuts(segment)[p]
                    here = pl.ds(lo, n)
                    part[slot, left, here] = part[slot, left, here] + rsrecv[slot, q - 1, here]
            send_stage(slot, c, stage + 1, send, recv)

    def sum_sent(c, send):
        for p in range(bits):
            lo, n = cuts(segment)[p]
            for q in range(1, op_size):
                wait(rsrecv.at[0, q - 1, pl.ds(lo, n)], send.at[c, q - 1, p])

    def own_total(slot, at, n):
        here = pl.ds(at, n)
        total = part[slot, 0, here]
        for b in range(bits):
            total = total + rsrecv[slot, (1 << b) - 1, here]
        return total

    def hand_out(c, copy, have):
        for p in range(bits):
            order = orders[p][::-1]
            for q in range(1, op_size):
                last = max(i for i, b in enumerate(order) if q >> b & 1)
                source = q ^ (1 << order[last])
                if source in have:
                    copy(c, p, source, q, 1 << order[last])

    waves = [[q for q in range(op_size) if bin(q).count("1") == n] for n in range(bits + 1)]

    def beta_first(c, start, end):
        @loop(end, start)
        def _(d):
            ysend[c, d] = beta(field, peer(d) * chunks + c, rows)

            @pl.when(d > 0)
            def _():
                to_peer(ysend.at[c, d], yrecv.at[c, d - 1], y_send.at[c], y_recv.at[c], d)

                @pl.when(c + 1 < chunks)
                def _():
                    send_previous(c + 1, d)

    def keep(at_block, x):
        high, low = split(x)
        small[at_block, :block] = high
        small[at_block, block:] = low

    def pieces(h):
        for t in range(block // thin):
            g = h * block + t * thin
            yield g // piece, g % piece, t * thin

    def alpha_first(c):
        slot = lax.rem(c, 2)
        for h in range(chunks):
            keep(me * chunks + h, ysend[c, 0, h * block : (h + 1) * block])

        @loop(shards, 1)
        def _(d):
            for h in range(chunks):
                keep(peer(d) * chunks + h, yrecv[c, d - 1, h * block : (h + 1) * block])

        @pl.when(c >= 2)
        def _():
            sum_sent(c - 2, r1_send)

        @loop(shards)
        def _(d):
            for h in range(chunks):
                value = scale * alpha(
                    lambda b: [small[b, :block], small[b, block:]], peer(d) * chunks + h
                )
                for owner, at, start in pieces(h):
                    here = pl.ds(pl.multiple_of(d * piece + at, thin), thin)
                    part[slot, mate(owner), here] = value[start : start + thin]

        send_stage(slot, c, 0, r1_send, r1_recv)

    def hand_first(c, p, source, q, across):
        lo, n = cuts(segment)[p]
        to_mate(
            ufull.at[c, source, pl.ds(lo, n)], ufull.at[c, q, pl.ds(lo, n)],
            g1_send.at[c, q - 1, p], g1_recv.at[c, q - 1, p], across,
        )

    def handed_first(c, sem, slots_):
        for p in range(bits):
            lo, n = cuts(segment)[p]
            for q in slots_:
                wait(ufull.at[c, q, pl.ds(lo, n)], sem.at[c, q - 1, p])

    def add_first(c):
        slot = lax.rem(c, 2)
        relay_stages(slot, c, r1_send, r1_recv)

        @pl.when(c == 0)
        def _():
            q_copy.start()

        wait(precv.at[c, pl.ds(1, shards - 1)], p_recv.at[c])
        arrived(slot, c, bits - 1, r1_recv)

        @loop(shards)
        def _(d):
            at = pl.multiple_of(d * piece, piece)
            ufull[c, 0, pl.ds(at, piece)] = own_total(slot, at, piece) - precv[c, d]

        hand_out(c, hand_first, waves[0])

    def alpha_piece(r, c, start, end):
        at = pl.multiple_of(r * block, block)
        column = pl.multiple_of(2 * block * c, 2 * block)

        @loop(end, start)
        def _(d):
            ysend[c, d, pl.ds(at, block)] = alpha(
                lambda b: [
                    field[b, pl.ds(column, block)],
                    field[b, pl.ds(column + block, block)],
                ],
                peer(d) * chunks + r,
            )

            @pl.when(d > 0)
            def _():
                to_peer(
                    ysend.at[c, d, pl.ds(at, block)], wrecv.at[r, c, d - 1],
                    w_send.at[r], w_recv.at[r], d,
                )

    def relay_first(c):
        for wave in waves[1:-1]:
            handed_first(c, g1_recv, wave)
            hand_out(c, hand_first, wave)

    def alpha_second(c):
        handed_first(c, g1_recv, waves[-1])
        column = pl.multiple_of(2 * block * c, 2 * block)

        @loop(shards)
        def _(d):
            for h in range(chunks):
                x = jnp.concatenate(
                    [
                        ufull[c, mate(owner), pl.ds(pl.multiple_of(d * piece + at, thin), thin)]
                        for owner, at, _ in pieces(h)
                    ],
                    axis=0,
                )
                high, low = split(x)
                field[peer(d) * chunks + h, pl.ds(column, block)] = high
                field[peer(d) * chunks + h, pl.ds(column + block, block)] = low

        wait(yrecv.at[c], y_send.at[c])

        @loop(early)
        def _(r):
            alpha_piece(r, c, 0, shards)

    beta_first(0, 0, shards)
    if chunks > 1:
        beta_first(1, 0, near)

    @loop(chunks)
    def _(c):
        wait(yrecv.at[c], y_recv.at[c])

        @pl.when(c + 1 < chunks)
        def _():
            beta_first(c + 1, near, shards)

        @pl.when(c + 2 < chunks)
        def _():
            beta_first(c + 2, 0, near)

        alpha_first(c)

        @pl.when(c == chunks - 1)
        def _():
            loop(chunks - 1)(alpha_second)

        add_first(c)
        relay_first(c)

    alpha_second(chunks - 1)

    @loop((chunks - early) * chunks)
    def _(i):
        alpha_piece(early + lax.div(i, chunks), lax.rem(i, chunks), 0, near)

    def send_far(r):
        loop(chunks)(lambda c: alpha_piece(r, c, near, shards))

    for c in range(max(0, chunks - 2), chunks):
        sum_sent(c, r1_send)
    for c in range(chunks):
        handed_first(c, g1_send, range(1, op_size))
    q_copy.wait()

    def row_block(r):
        return pl.ds(pl.multiple_of(r * block, block), block)

    def beta_second(r):
        slot = lax.rem(r, 2)
        at = row_block(r)
        wait(wrecv.at[r], w_recv.at[r])

        @pl.when(jnp.logical_and(r >= early, r + 1 < chunks))
        def _():
            send_far(r + 1)

        for c in range(chunks):
            keep(me * chunks + c, ysend[c, 0, at])

        @loop(shards, 1)
        def _(d):
            for c in range(chunks):
                keep(peer(d) * chunks + c, wrecv[r, c, d - 1])

        @pl.when(r >= 2)
        def _():
            sum_sent(r - 2, r2_send)

        group = math.gcd(share, 4)

        @loop(blocks // group)
        def _(i):
            for g in range(group):
                b = i * group + g
                here = pl.ds(pl.multiple_of(lax.rem(b, share) * block, block), block)
                part[slot, mate(lax.div(b, share)), here] = scale * beta(small, b, block)

        send_stage(slot, r, 0, r2_send, r2_recv)

        @pl.when(r == 0)
        def _():
            if early < chunks:
                send_far(early)


    def out_part(r, p, q):
        lo, n = cuts(block)[p]
        here = pl.ds(pl.multiple_of(r * block + lo, 8), n)
        return out_hbm.at[here, pl.ds(pl.multiple_of(mate(q) * segment, segment), segment)]

    def hand_second(r, p, source, q, across):
        lo, n = cuts(block)[p]
        own = vq.at[pl.ds(pl.multiple_of(r * block + lo, 8), n)]
        there = out_part(r, p, source)
        to_mate(
            there if source else own, there,
            g2_send.at[r, q - 1, p], g2_recv.at[r, q - 1, p], across,
        )

    def add_second(r):
        slot = lax.rem(r, 2)
        at = row_block(r)
        arrived(slot, r, bits - 1, r2_recv)
        for j in range(share):
            columns = pl.ds(j * block, block)
            vq[at, columns] = own_total(slot, j * block, block) - vq[at, columns]
        hand_out(r, hand_second, waves[0])
        pltpu.make_async_copy(vq.at[at], out_hbm.at[at, quarter], o_sem.at[r]).start()

    def handed_second(r, sem, slots_):
        for p in range(bits):
            for q in slots_:
                wait(out_part(r, p, q), sem.at[r, q - 1, p])

    def relay_second(r):
        for wave in waves[1:]:
            handed_second(r, g2_recv, wave)
            hand_out(r, hand_second, wave)

    acts = {
        "beta": beta_second,
        "relay": lambda r: relay_stages(lax.rem(r, 2), r, r2_send, r2_recv),
        "add": add_second,
        "hand": relay_second,
    }
    pair = range(min(2, chunks))
    order = [(act, r) for act in ("beta", "relay", "add", "hand") for r in pair]
    for r in range(2, chunks):
        at = len(order) - 1
        order.insert(at, ("beta", r))
        order += [(act, r) for act in ("relay", "add", "hand")]

    @loop(len(order))
    def _(t):
        for name, act in acts.items():
            ticks = [order.index((name, r)) for r in range(chunks)]
            now = functools.reduce(jnp.logical_or, [t == k for k in ticks])
            r = sum(jnp.minimum(jnp.maximum(t - k + 1, 0), 1) for k in ticks) - 1

            @pl.when(now)
            def _():
                act(r)

    for r in range(chunks):
        handed_second(r, g2_send, range(1, op_size))
        wait(vq.at[pl.ds(r * block, block)], o_sem.at[r])
        wait(wrecv.at[r], w_send.at[r])
        wait(precv.at[r, pl.ds(1, shards - 1)], p_send.at[r])
    for r in range(max(0, chunks - 2), chunks):
        sum_sent(r, r2_send)


def per_device(coeffs, previous, block_values, block_cols):
    op_size, shards = lax.axis_size("op"), lax.axis_size("str")
    scale = 2.0 / math.sqrt(block_values.shape[0] * op_size)
    values = block_values[0]
    cols = block_cols[0].reshape(-1)
    blocks, slots, block, _ = values.shape
    rows, width = coeffs.shape
    chunks = blocks // shards
    piece = rows // op_size
    segment = width // op_size
    paths = (chunks, op_size - 1, max(1, op_size.bit_length() - 1))
    vmem, dma = pltpu.VMEM, pltpu.SemaphoreType.DMA
    anywhere = pl.BlockSpec(memory_space=pl.ANY)
    return pl.pallas_call(
        functools.partial(body, shards, op_size, slots, block, chunks, scale),
        out_shape=jax.ShapeDtypeStruct((rows, width), F32),
        in_specs=[pl.BlockSpec(memory_space=pltpu.SMEM), anywhere, anywhere, anywhere],
        out_specs=anywhere,
        scratch_shapes=[
            vmem((blocks, slots, block, block), BF16),
            vmem((blocks, 2 * rows, block), BF16),
            vmem((chunks, shards, rows, block), F32),
            vmem((chunks, shards - 1, rows, block), F32),
            vmem((chunks, chunks, shards - 1, block, block), F32),
            vmem((chunks, shards, piece, block), F32),
            vmem((blocks, 2 * block, block), BF16),
            vmem((2, op_size, segment, block), F32),
            vmem((chunks, op_size, segment, block), F32),
            vmem((2, op_size - 1, segment, block), F32),
            vmem((2, rows, rows), F32),
            vmem((rows, segment), F32),
            dma, dma((2,)), dma, dma((chunks,)),
            dma((chunks,)), dma((chunks,)), dma((chunks,)), dma((chunks,)),
            dma(paths), dma(paths), dma(paths), dma(paths),
            dma((chunks,)), dma((chunks,)),
            dma(paths), dma(paths), dma(paths), dma(paths),
        ],
        compiler_params=pltpu.CompilerParams(
            collective_id=0, has_side_effects=True, vmem_limit_bytes=VMEM_LIMIT
        ),
        cost_estimate=pl.CostEstimate(
            flops=16 * blocks * slots * block * block * rows,
            bytes_accessed=32 * rows * width,
            transcendentals=0,
        ),
    )(cols, values, coeffs, previous)


def solution(mesh):
    placed = (P("str", None), P("str", None), P("op", None, None, None, None), P("op", None, None))
    return jax.shard_map(
        per_device, mesh=mesh, in_specs=placed, out_specs=P("str", None), check_vma=False
    )
```

```python
import functools
import math

import jax
import jax.numpy as jnp
from jax import lax
from jax.experimental import pallas as pl
from jax.experimental.pallas import tpu as pltpu
from jax.sharding import PartitionSpec as P

F32, BF16 = jnp.float32, jnp.bfloat16
VMEM_LIMIT = 67_043_328


def split(x):
    high = x.astype(BF16)
    return high, (x - high.astype(F32)).astype(BF16)


def flip(a, b, size):
    total, bit = 0, 1
    while bit < size:
        total = total + bit * lax.rem(lax.div(a, bit) + lax.div(b, bit), 2)
        bit *= 2
    return total


def body(
    shards, op_size, slots, block, chunks, scale,
    cols_ref, a_hbm, v_hbm, p_hbm, out_hbm,
    a_ref, field, ysend, yrecv, wrecv, precv, small, part, ufull, rsrecv, vstage, vq,
    a_sem, v_sem, q_sem, o_sem,
    y_send, y_recv, p_send, p_recv, r1_send, r1_recv, g1_send, g1_recv,
    w_send, w_recv, r2_send, r2_recv, g2_send, g2_recv,
):
    blocks = chunks * shards
    rows = chunks * block
    piece = rows // op_size
    thin = min(block, piece)
    wide = rows
    share = blocks // op_size
    segment = share * block
    early = max(1, chunks // 2)
    near = max(1, shards // 2)
    bits = max(1, op_size.bit_length() - 1)
    i32 = jnp.int32
    me, op = lax.axis_index("str").astype(i32), lax.axis_index("op").astype(i32)

    def cuts(n):
        marks = [n * p // bits // 8 * 8 for p in range(bits)] + [n]
        return [(marks[p], marks[p + 1] - marks[p]) for p in range(bits)]

    def first_bit(q, order):
        return next(i for i, b in enumerate(order) if q >> b & 1)

    orders = [[(p + i) % bits for i in range(bits)] for p in range(bits)]
    stages = [
        [
            (p, q, orders[p][i])
            for p in range(bits)
            for q in range(1, op_size)
            if first_bit(q, orders[p]) == i
        ]
        for i in range(bits)
    ]

    def peer(d):
        return flip(me, jnp.asarray(d, i32), shards)

    def mate(q):
        return flip(op, jnp.asarray(q, i32), op_size)

    def wait(ref, sem):
        pltpu.make_async_copy(ref, ref, sem).wait()

    def to_peer(src, dst, send, recv, d):
        pltpu.make_async_remote_copy(
            src_ref=src, dst_ref=dst, send_sem=send, recv_sem=recv,
            device_id={"str": peer(d)}, device_id_type=pl.DeviceIdType.MESH,
        ).start()

    def to_mate(src, dst, send, recv, q):
        pltpu.make_async_remote_copy(
            src_ref=src, dst_ref=dst, send_sem=send, recv_sem=recv,
            device_id={"op": mate(q)}, device_id_type=pl.DeviceIdType.MESH,
        ).start()

    def loop(n, start=0):
        def run(step):
            lax.fori_loop(start, n, lambda i, _: (step(i), None)[1], None)
        return run

    def v_copy(g):
        return pltpu.make_async_copy(
            v_hbm.at[:, pl.ds(pl.multiple_of(g * wide, block), wide)],
            vstage.at[lax.rem(g, 2)],
            v_sem.at[lax.rem(g, 2)],
        )

    def p_part(c, d):
        at = pl.multiple_of((peer(d) * chunks + c) * block, block)
        return p_hbm.at[pl.ds(pl.multiple_of(op * piece, piece), piece), pl.ds(at, block)]

    def send_previous(c, d):
        to_peer(p_part(c, d), precv.at[c, d], p_send.at[c], p_recv.at[c], d)

    a_copy = pltpu.make_async_copy(a_hbm, a_ref, a_sem)
    quarter = pl.ds(pl.multiple_of(op * segment, block), segment)
    q_copy = pltpu.make_async_copy(v_hbm.at[:, quarter], vq, q_sem)

    v_copy(jnp.int32(0)).start()
    a_copy.start()

    barrier = pltpu.get_barrier_semaphore()
    for d in range(1, shards):
        pl.semaphore_signal(
            barrier, inc=1, device_id={"str": peer(d)}, device_id_type=pl.DeviceIdType.MESH
        )
    for q in range(1, op_size):
        pl.semaphore_signal(
            barrier, inc=1, device_id={"op": mate(q)}, device_id_type=pl.DeviceIdType.MESH
        )

    for c in range(chunks):
        pltpu.make_async_copy(p_part(c, 0), precv.at[c, 0], o_sem.at[c]).start()
    pl.semaphore_wait(barrier, shards - 1 + op_size - 1)

    @loop(shards, 1)
    def _(d):
        send_previous(0, d)

    @loop(shards)
    def _(g):
        @pl.when(g + 1 < shards)
        def _():
            v_copy(g + 1).start()

        v_copy(g).wait()
        for i in range(chunks):
            high, low = split(vstage[lax.rem(g, 2), :, i * block : (i + 1) * block])
            field[g * chunks + i, :rows] = high
            field[g * chunks + i, rows:] = low

    a_copy.wait()
    for c in range(chunks):
        wait(precv.at[c, 0], o_sem.at[c])

    def operator_row(row):
        return jnp.concatenate([a_ref[row, j] for j in range(slots)], axis=1)

    def beta(source, row, m):
        left = jnp.concatenate(
            [source[cols_ref[row * slots + j]] for j in range(slots)], axis=1
        )
        both = lax.dot_general(
            left, operator_row(row), (((1,), (1,)), ((), ())), preferred_element_type=F32
        )
        return both[:m] + both[m:]

    def alpha(load, row):
        right = jnp.concatenate(
            [
                jnp.concatenate(load(cols_ref[row * slots + j]), axis=1)
                for j in range(slots)
            ],
            axis=0,
        )
        both = jnp.dot(operator_row(row), right, preferred_element_type=F32)
        return both[:, :block] + both[:, block:]

    def send_stage(slot, c, stage, send, recv):
        for p, q, b in stages[stage]:
            lo, n = cuts(segment)[p]
            to_mate(
                part.at[slot, q, pl.ds(lo, n)], rsrecv.at[slot, q - 1, pl.ds(lo, n)],
                send.at[c, q - 1, p], recv.at[c, q - 1, p], 1 << b,
            )

    def arrived(slot, c, stage, recv):
        for p, q, b in stages[stage]:
            lo, n = cuts(segment)[p]
            wait(rsrecv.at[slot, q - 1, pl.ds(lo, n)], recv.at[c, q - 1, p])

    def relay_stages(slot, c, send, recv):
        for stage in range(bits - 1):
            arrived(slot, c, stage, recv)
            for p, q, b in stages[stage]:
                left = q ^ (1 << b)
                if left:
                    lo, n = cuts(segment)[p]
                    here = pl.ds(lo, n)
                    part[slot, left, here] = part[slot, left, here] + rsrecv[slot, q - 1, here]
            send_stage(slot, c, stage + 1, send, recv)

    def sum_sent(c, send):
        for p in range(bits):
            lo, n = cuts(segment)[p]
            for q in range(1, op_size):
                wait(rsrecv.at[0, q - 1, pl.ds(lo, n)], send.at[c, q - 1, p])

    def own_total(slot, at, n):
        here = pl.ds(at, n)
        total = part[slot, 0, here]
        for b in range(bits):
            total = total + rsrecv[slot, (1 << b) - 1, here]
        return total

    def hand_out(c, copy, have):
        for p in range(bits):
            order = orders[p][::-1]
            for q in range(1, op_size):
                last = max(i for i, b in enumerate(order) if q >> b & 1)
                source = q ^ (1 << order[last])
                if source in have:
                    copy(c, p, source, q, 1 << order[last])

    waves = [[q for q in range(op_size) if bin(q).count("1") == n] for n in range(bits + 1)]

    def beta_first(c, start, end):
        @loop(end, start)
        def _(d):
            ysend[c, d] = beta(field, peer(d) * chunks + c, rows)

            @pl.when(d > 0)
            def _():
                to_peer(ysend.at[c, d], yrecv.at[c, d - 1], y_send.at[c], y_recv.at[c], d)

                @pl.when(c + 1 < chunks)
                def _():
                    send_previous(c + 1, d)

    def keep(at_block, x):
        high, low = split(x)
        small[at_block, :block] = high
        small[at_block, block:] = low

    def pieces(h):
        for t in range(block // thin):
            g = h * block + t * thin
            yield g // piece, g % piece, t * thin

    def alpha_first(c):
        slot = lax.rem(c, 2)
        for h in range(chunks):
            keep(me * chunks + h, ysend[c, 0, h * block : (h + 1) * block])

        @loop(shards, 1)
        def _(d):
            for h in range(chunks):
                keep(peer(d) * chunks + h, yrecv[c, d - 1, h * block : (h + 1) * block])

        @pl.when(c >= 2)
        def _():
            sum_sent(c - 2, r1_send)

        @loop(shards)
        def _(d):
            for h in range(chunks):
                value = scale * alpha(
                    lambda b: [small[b, :block], small[b, block:]], peer(d) * chunks + h
                )
                for owner, at, start in pieces(h):
                    here = pl.ds(pl.multiple_of(d * piece + at, thin), thin)
                    part[slot, mate(owner), here] = value[start : start + thin]

        send_stage(slot, c, 0, r1_send, r1_recv)

    def hand_first(c, p, source, q, across):
        lo, n = cuts(segment)[p]
        to_mate(
            ufull.at[c, source, pl.ds(lo, n)], ufull.at[c, q, pl.ds(lo, n)],
            g1_send.at[c, q - 1, p], g1_recv.at[c, q - 1, p], across,
        )

    def handed_first(c, sem, slots_):
        for p in range(bits):
            lo, n = cuts(segment)[p]
            for q in slots_:
                wait(ufull.at[c, q, pl.ds(lo, n)], sem.at[c, q - 1, p])

    def add_first(c):
        slot = lax.rem(c, 2)
        relay_stages(slot, c, r1_send, r1_recv)

        @pl.when(c == 0)
        def _():
            q_copy.start()

        wait(precv.at[c, pl.ds(1, shards - 1)], p_recv.at[c])
        arrived(slot, c, bits - 1, r1_recv)

        @loop(shards)
        def _(d):
            at = pl.multiple_of(d * piece, piece)
            ufull[c, 0, pl.ds(at, piece)] = own_total(slot, at, piece) - precv[c, d]

        hand_out(c, hand_first, waves[0])

    def alpha_piece(r, c, start, end):
        at = pl.multiple_of(r * block, block)
        column = pl.multiple_of(2 * block * c, 2 * block)

        @loop(end, start)
        def _(d):
            ysend[c, d, pl.ds(at, block)] = alpha(
                lambda b: [
                    field[b, pl.ds(column, block)],
                    field[b, pl.ds(column + block, block)],
                ],
                peer(d) * chunks + r,
            )

            @pl.when(d > 0)
            def _():
                to_peer(
                    ysend.at[c, d, pl.ds(at, block)], wrecv.at[r, c, d - 1],
                    w_send.at[r], w_recv.at[r], d,
                )

    def relay_first(c):
        for wave in waves[1:-1]:
            handed_first(c, g1_recv, wave)
            hand_out(c, hand_first, wave)

    def alpha_second(c):
        handed_first(c, g1_recv, waves[-1])
        column = pl.multiple_of(2 * block * c, 2 * block)

        @loop(shards)
        def _(d):
            for h in range(chunks):
                x = jnp.concatenate(
                    [
                        ufull[c, mate(owner), pl.ds(pl.multiple_of(d * piece + at, thin), thin)]
                        for owner, at, _ in pieces(h)
                    ],
                    axis=0,
                )
                high, low = split(x)
                field[peer(d) * chunks + h, pl.ds(column, block)] = high
                field[peer(d) * chunks + h, pl.ds(column + block, block)] = low

        wait(yrecv.at[c], y_send.at[c])

        @loop(early)
        def _(r):
            alpha_piece(r, c, 0, shards)

    beta_first(0, 0, shards)
    if chunks > 1:
        beta_first(1, 0, near)

    @loop(chunks)
    def _(c):
        wait(yrecv.at[c], y_recv.at[c])

        @pl.when(c + 1 < chunks)
        def _():
            beta_first(c + 1, near, shards)

        @pl.when(c + 2 < chunks)
        def _():
            beta_first(c + 2, 0, near)

        alpha_first(c)

        @pl.when(c == chunks - 1)
        def _():
            loop(chunks - 1)(alpha_second)

        add_first(c)
        relay_first(c)

    alpha_second(chunks - 1)

    @loop((chunks - early) * chunks)
    def _(i):
        alpha_piece(early + lax.div(i, chunks), lax.rem(i, chunks), 0, near)

    half = chunks // 2

    def send_far(r, start, end):
        loop(end, start)(lambda c: alpha_piece(r, c, near, shards))

    if early < chunks:
        send_far(early, 0, half)

    for c in range(max(0, chunks - 2), chunks):
        sum_sent(c, r1_send)
    for c in range(chunks):
        handed_first(c, g1_send, range(1, op_size))
    q_copy.wait()

    def row_block(r):
        return pl.ds(pl.multiple_of(r * block, block), block)

    def beta_second(r):
        slot = lax.rem(r, 2)
        at = row_block(r)
        wait(wrecv.at[r], w_recv.at[r])

        @pl.when(jnp.logical_and(r >= early, r + 1 < chunks))
        def _():
            send_far(r + 1, half, chunks)

        if early + 2 < chunks:
            @pl.when(jnp.logical_and(r >= early, r + 2 < chunks))
            def _():
                send_far(r + 2, 0, half)

        for c in range(chunks):
            keep(me * chunks + c, ysend[c, 0, at])

        @loop(shards, 1)
        def _(d):
            for c in range(chunks):
                keep(peer(d) * chunks + c, wrecv[r, c, d - 1])

        @pl.when(r >= 2)
        def _():
            sum_sent(r - 2, r2_send)

        group = math.gcd(share, 4)

        @loop(blocks // group)
        def _(i):
            for g in range(group):
                b = i * group + g
                here = pl.ds(pl.multiple_of(lax.rem(b, share) * block, block), block)
                part[slot, mate(lax.div(b, share)), here] = scale * beta(small, b, block)

        send_stage(slot, r, 0, r2_send, r2_recv)

        @pl.when(r == 0)
        def _():
            if early < chunks:
                send_far(early, half, chunks)
            if early + 1 < chunks:
                send_far(early + 1, 0, half)


    def out_part(r, p, q):
        lo, n = cuts(block)[p]
        here = pl.ds(pl.multiple_of(r * block + lo, 8), n)
        return out_hbm.at[here, pl.ds(pl.multiple_of(mate(q) * segment, segment), segment)]

    def hand_second(r, p, source, q, across):
        lo, n = cuts(block)[p]
        own = vq.at[pl.ds(pl.multiple_of(r * block + lo, 8), n)]
        there = out_part(r, p, source)
        to_mate(
            there if source else own, there,
            g2_send.at[r, q - 1, p], g2_recv.at[r, q - 1, p], across,
        )

    def add_second(r):
        slot = lax.rem(r, 2)
        at = row_block(r)
        arrived(slot, r, bits - 1, r2_recv)
        for j in range(share):
            columns = pl.ds(j * block, block)
            vq[at, columns] = own_total(slot, j * block, block) - vq[at, columns]
        hand_out(r, hand_second, waves[0])
        pltpu.make_async_copy(vq.at[at], out_hbm.at[at, quarter], o_sem.at[r]).start()

    def handed_second(r, sem, slots_):
        for p in range(bits):
            for q in slots_:
                wait(out_part(r, p, q), sem.at[r, q - 1, p])

    def relay_second(r):
        for wave in waves[1:-1]:
            handed_second(r, g2_recv, wave)
            hand_out(r, hand_second, wave)

    acts = {
        "beta": beta_second,
        "relay": lambda r: relay_stages(lax.rem(r, 2), r, r2_send, r2_recv),
        "add": add_second,
        "hand": relay_second,
    }
    order = [(act, r) for r in range(min(2, chunks)) for act in ("beta", "relay")]
    order += [(act, r) for act in ("add", "hand") for r in range(min(2, chunks))]
    for r in range(2, chunks):
        order.insert(len(order) - (r == 2), ("beta", r))
        order += [(act, r) for act in ("relay", "add", "hand")]

    @loop(len(order))
    def _(t):
        for name, act in acts.items():
            ticks = [order.index((name, r)) for r in range(chunks)]
            now = functools.reduce(jnp.logical_or, [t == k for k in ticks])
            r = sum(jnp.minimum(jnp.maximum(t - k + 1, 0), 1) for k in ticks) - 1

            @pl.when(now)
            def _():
                act(r)

    for r in range(chunks):
        handed_second(r, g2_recv, waves[-1])
        handed_second(r, g2_send, range(1, op_size))
        wait(vq.at[pl.ds(r * block, block)], o_sem.at[r])
        wait(wrecv.at[r], w_send.at[r])
        wait(precv.at[r, pl.ds(1, shards - 1)], p_send.at[r])
    for r in range(max(0, chunks - 2), chunks):
        sum_sent(r, r2_send)


def per_device(coeffs, previous, block_values, block_cols):
    op_size, shards = lax.axis_size("op"), lax.axis_size("str")
    scale = 2.0 / math.sqrt(block_values.shape[0] * op_size)
    values = block_values[0]
    cols = block_cols[0].reshape(-1)
    blocks, slots, block, _ = values.shape
    rows, width = coeffs.shape
    chunks = blocks // shards
    piece = rows // op_size
    segment = width // op_size
    paths = (chunks, op_size - 1, max(1, op_size.bit_length() - 1))
    vmem, dma = pltpu.VMEM, pltpu.SemaphoreType.DMA
    anywhere = pl.BlockSpec(memory_space=pl.ANY)
    return pl.pallas_call(
        functools.partial(body, shards, op_size, slots, block, chunks, scale),
        out_shape=jax.ShapeDtypeStruct((rows, width), F32),
        in_specs=[pl.BlockSpec(memory_space=pltpu.SMEM), anywhere, anywhere, anywhere],
        out_specs=anywhere,
        scratch_shapes=[
            vmem((blocks, slots, block, block), BF16),
            vmem((blocks, 2 * rows, block), BF16),
            vmem((chunks, shards, rows, block), F32),
            vmem((chunks, shards - 1, rows, block), F32),
            vmem((chunks, chunks, shards - 1, block, block), F32),
            vmem((chunks, shards, piece, block), F32),
            vmem((blocks, 2 * block, block), BF16),
            vmem((2, op_size, segment, block), F32),
            vmem((chunks, op_size, segment, block), F32),
            vmem((2, op_size - 1, segment, block), F32),
            vmem((2, rows, rows), F32),
            vmem((rows, segment), F32),
            dma, dma((2,)), dma, dma((chunks,)),
            dma((chunks,)), dma((chunks,)), dma((chunks,)), dma((chunks,)),
            dma(paths), dma(paths), dma(paths), dma(paths),
            dma((chunks,)), dma((chunks,)),
            dma(paths), dma(paths), dma(paths), dma(paths),
        ],
        compiler_params=pltpu.CompilerParams(
            collective_id=0, has_side_effects=True, vmem_limit_bytes=VMEM_LIMIT
        ),
        cost_estimate=pl.CostEstimate(
            flops=16 * blocks * slots * block * block * rows,
            bytes_accessed=32 * rows * width,
            transcendentals=0,
        ),
    )(cols, values, coeffs, previous)


def solution(mesh):
    placed = (P("str", None), P("str", None), P("op", None, None, None, None), P("op", None, None))
    return jax.shard_map(
        per_device, mesh=mesh, in_specs=placed, out_specs=P("str", None), check_vma=False
    )
```

```python
import functools
import math

import jax
import jax.numpy as jnp
from jax import lax
from jax.experimental import pallas as pl
from jax.experimental.pallas import tpu as pltpu
from jax.sharding import PartitionSpec as P

F32, BF16 = jnp.float32, jnp.bfloat16
VMEM_LIMIT = 67_043_328


def split(x):
    high = x.astype(BF16)
    return high, (x - high.astype(F32)).astype(BF16)


def flip(a, b, size):
    total, bit = 0, 1
    while bit < size:
        total = total + bit * lax.rem(lax.div(a, bit) + lax.div(b, bit), 2)
        bit *= 2
    return total


def body(
    shards, op_size, slots, block, chunks, scale,
    cols_ref, a_hbm, v_hbm, p_hbm, out_hbm,
    a_ref, field, ysend, yrecv, wrecv, precv, small, part, ufull, rsrecv, vstage, vq,
    a_sem, v_sem, q_sem, o_sem,
    y_send, y_recv, p_send, p_recv, r1_send, r1_recv, g1_send, g1_recv,
    w_send, w_recv, r2_send, r2_recv, g2_send, g2_recv,
):
    blocks = chunks * shards
    rows = chunks * block
    piece = rows // op_size
    thin = min(block, piece)
    wide = rows
    share = blocks // op_size
    segment = share * block
    early = max(1, chunks // 2)
    near = max(1, shards // 2)
    bits = max(1, op_size.bit_length() - 1)
    i32 = jnp.int32
    me, op = lax.axis_index("str").astype(i32), lax.axis_index("op").astype(i32)

    def cuts(n):
        marks = [n * p // bits // 8 * 8 for p in range(bits)] + [n]
        return [(marks[p], marks[p + 1] - marks[p]) for p in range(bits)]

    def first_bit(q, order):
        return next(i for i, b in enumerate(order) if q >> b & 1)

    orders = [[(p + i) % bits for i in range(bits)] for p in range(bits)]
    stages = [
        [
            (p, q, orders[p][i])
            for p in range(bits)
            for q in range(1, op_size)
            if first_bit(q, orders[p]) == i
        ]
        for i in range(bits)
    ]

    def peer(d):
        return flip(me, jnp.asarray(d, i32), shards)

    def mate(q):
        return flip(op, jnp.asarray(q, i32), op_size)

    def wait(ref, sem):
        pltpu.make_async_copy(ref, ref, sem).wait()

    def to_peer(src, dst, send, recv, d):
        pltpu.make_async_remote_copy(
            src_ref=src, dst_ref=dst, send_sem=send, recv_sem=recv,
            device_id={"str": peer(d)}, device_id_type=pl.DeviceIdType.MESH,
        ).start()

    def to_mate(src, dst, send, recv, q):
        pltpu.make_async_remote_copy(
            src_ref=src, dst_ref=dst, send_sem=send, recv_sem=recv,
            device_id={"op": mate(q)}, device_id_type=pl.DeviceIdType.MESH,
        ).start()

    def loop(n, start=0):
        def run(step):
            lax.fori_loop(start, n, lambda i, _: (step(i), None)[1], None)
        return run

    def v_copy(g):
        return pltpu.make_async_copy(
            v_hbm.at[:, pl.ds(pl.multiple_of(g * wide, block), wide)],
            vstage.at[lax.rem(g, 2)],
            v_sem.at[lax.rem(g, 2)],
        )

    def p_part(c, d):
        at = pl.multiple_of((peer(d) * chunks + c) * block, block)
        return p_hbm.at[pl.ds(pl.multiple_of(op * piece, piece), piece), pl.ds(at, block)]

    def send_previous(c, d):
        to_peer(p_part(c, d), precv.at[c, d], p_send.at[c], p_recv.at[c], d)

    a_copy = pltpu.make_async_copy(a_hbm, a_ref, a_sem)
    quarter = pl.ds(pl.multiple_of(op * segment, block), segment)
    q_copy = pltpu.make_async_copy(v_hbm.at[:, quarter], vq, q_sem)

    v_copy(jnp.int32(0)).start()
    a_copy.start()

    barrier = pltpu.get_barrier_semaphore()
    for d in range(1, shards):
        pl.semaphore_signal(
            barrier, inc=1, device_id={"str": peer(d)}, device_id_type=pl.DeviceIdType.MESH
        )
    for q in range(1, op_size):
        pl.semaphore_signal(
            barrier, inc=1, device_id={"op": mate(q)}, device_id_type=pl.DeviceIdType.MESH
        )

    for c in range(chunks):
        pltpu.make_async_copy(p_part(c, 0), precv.at[c, 0], o_sem.at[c]).start()
    pl.semaphore_wait(barrier, shards - 1 + op_size - 1)

    @loop(shards, 1)
    def _(d):
        send_previous(0, d)

    @loop(shards)
    def _(g):
        @pl.when(g + 1 < shards)
        def _():
            v_copy(g + 1).start()

        v_copy(g).wait()
        for i in range(chunks):
            high, low = split(vstage[lax.rem(g, 2), :, i * block : (i + 1) * block])
            field[g * chunks + i, :rows] = high
            field[g * chunks + i, rows:] = low

    a_copy.wait()
    for c in range(chunks):
        wait(precv.at[c, 0], o_sem.at[c])

    def operator_row(row):
        return jnp.concatenate([a_ref[row, j] for j in range(slots)], axis=1)

    def beta(source, row, m):
        left = jnp.concatenate(
            [source[cols_ref[row * slots + j]] for j in range(slots)], axis=1
        )
        both = lax.dot_general(
            left, operator_row(row), (((1,), (1,)), ((), ())), preferred_element_type=F32
        )
        return both[:m] + both[m:]

    def alpha(load, row):
        right = jnp.concatenate(
            [
                jnp.concatenate(load(cols_ref[row * slots + j]), axis=1)
                for j in range(slots)
            ],
            axis=0,
        )
        both = jnp.dot(operator_row(row), right, preferred_element_type=F32)
        return both[:, :block] + both[:, block:]

    def send_stage(slot, c, stage, send, recv):
        for p, q, b in stages[stage]:
            lo, n = cuts(segment)[p]
            to_mate(
                part.at[slot, q, pl.ds(lo, n)], rsrecv.at[slot, q - 1, pl.ds(lo, n)],
                send.at[c, q - 1, p], recv.at[c, q - 1, p], 1 << b,
            )

    def arrived(slot, c, stage, recv):
        for p, q, b in stages[stage]:
            lo, n = cuts(segment)[p]
            wait(rsrecv.at[slot, q - 1, pl.ds(lo, n)], recv.at[c, q - 1, p])

    def relay_stages(slot, c, send, recv):
        for stage in range(bits - 1):
            arrived(slot, c, stage, recv)
            for p, q, b in stages[stage]:
                left = q ^ (1 << b)
                if left:
                    lo, n = cuts(segment)[p]
                    here = pl.ds(lo, n)
                    part[slot, left, here] = part[slot, left, here] + rsrecv[slot, q - 1, here]
            send_stage(slot, c, stage + 1, send, recv)

    def sum_sent(c, send):
        for p in range(bits):
            lo, n = cuts(segment)[p]
            for q in range(1, op_size):
                wait(rsrecv.at[0, q - 1, pl.ds(lo, n)], send.at[c, q - 1, p])

    def own_total(slot, at, n):
        here = pl.ds(at, n)
        total = part[slot, 0, here]
        for b in range(bits):
            total = total + rsrecv[slot, (1 << b) - 1, here]
        return total

    def hand_out(c, copy, have):
        for p in range(bits):
            order = orders[p][::-1]
            for q in range(1, op_size):
                last = max(i for i, b in enumerate(order) if q >> b & 1)
                source = q ^ (1 << order[last])
                if source in have:
                    copy(c, p, source, q, 1 << order[last])

    waves = [[q for q in range(op_size) if bin(q).count("1") == n] for n in range(bits + 1)]

    def beta_first(c, start, end):
        @loop(end, start)
        def _(d):
            ysend[c, d] = beta(field, peer(d) * chunks + c, rows)

            @pl.when(d > 0)
            def _():
                to_peer(ysend.at[c, d], yrecv.at[c, d - 1], y_send.at[c], y_recv.at[c], d)

                @pl.when(c + 1 < chunks)
                def _():
                    send_previous(c + 1, d)

    def keep(at_block, x):
        high, low = split(x)
        small[at_block, :block] = high
        small[at_block, block:] = low

    def pieces(h):
        for t in range(block // thin):
            g = h * block + t * thin
            yield g // piece, g % piece, t * thin

    def alpha_first(c):
        slot = lax.rem(c, 2)
        for h in range(chunks):
            keep(me * chunks + h, ysend[c, 0, h * block : (h + 1) * block])

        @loop(shards, 1)
        def _(d):
            for h in range(chunks):
                keep(peer(d) * chunks + h, yrecv[c, d - 1, h * block : (h + 1) * block])

        @pl.when(c >= 2)
        def _():
            sum_sent(c - 2, r1_send)

        @loop(shards)
        def _(d):
            for h in range(chunks):
                value = scale * alpha(
                    lambda b: [small[b, :block], small[b, block:]], peer(d) * chunks + h
                )
                for owner, at, start in pieces(h):
                    here = pl.ds(pl.multiple_of(d * piece + at, thin), thin)
                    part[slot, mate(owner), here] = value[start : start + thin]

        send_stage(slot, c, 0, r1_send, r1_recv)

    def hand_first(c, p, source, q, across):
        lo, n = cuts(segment)[p]
        to_mate(
            ufull.at[c, source, pl.ds(lo, n)], ufull.at[c, q, pl.ds(lo, n)],
            g1_send.at[c, q - 1, p], g1_recv.at[c, q - 1, p], across,
        )

    def handed_first(c, sem, slots_):
        for p in range(bits):
            lo, n = cuts(segment)[p]
            for q in slots_:
                wait(ufull.at[c, q, pl.ds(lo, n)], sem.at[c, q - 1, p])

    def add_first(c):
        slot = lax.rem(c, 2)
        relay_stages(slot, c, r1_send, r1_recv)

        @pl.when(c == 0)
        def _():
            q_copy.start()

        wait(precv.at[c, pl.ds(1, shards - 1)], p_recv.at[c])
        arrived(slot, c, bits - 1, r1_recv)

        @loop(shards)
        def _(d):
            at = pl.multiple_of(d * piece, piece)
            ufull[c, 0, pl.ds(at, piece)] = own_total(slot, at, piece) - precv[c, d]

        hand_out(c, hand_first, waves[0])

    def alpha_piece(r, c, start, end):
        at = pl.multiple_of(r * block, block)
        column = pl.multiple_of(2 * block * c, 2 * block)

        @loop(end, start)
        def _(d):
            ysend[c, d, pl.ds(at, block)] = alpha(
                lambda b: [
                    field[b, pl.ds(column, block)],
                    field[b, pl.ds(column + block, block)],
                ],
                peer(d) * chunks + r,
            )

            @pl.when(d > 0)
            def _():
                to_peer(
                    ysend.at[c, d, pl.ds(at, block)], wrecv.at[r, c, d - 1],
                    w_send.at[r], w_recv.at[r], d,
                )

    def relay_first(c):
        for wave in waves[1:-1]:
            handed_first(c, g1_recv, wave)
            hand_out(c, hand_first, wave)

    def alpha_second(c):
        handed_first(c, g1_recv, waves[-1])
        column = pl.multiple_of(2 * block * c, 2 * block)

        @loop(shards)
        def _(d):
            for h in range(chunks):
                x = jnp.concatenate(
                    [
                        ufull[c, mate(owner), pl.ds(pl.multiple_of(d * piece + at, thin), thin)]
                        for owner, at, _ in pieces(h)
                    ],
                    axis=0,
                )
                high, low = split(x)
                field[peer(d) * chunks + h, pl.ds(column, block)] = high
                field[peer(d) * chunks + h, pl.ds(column + block, block)] = low

        wait(yrecv.at[c], y_send.at[c])

        @loop(early)
        def _(r):
            alpha_piece(r, c, 0, shards)

    beta_first(0, 0, shards)
    if chunks > 1:
        beta_first(1, 0, near)

    @loop(chunks)
    def _(c):
        wait(yrecv.at[c], y_recv.at[c])

        @pl.when(c + 1 < chunks)
        def _():
            beta_first(c + 1, near, shards)

        @pl.when(c + 2 < chunks)
        def _():
            beta_first(c + 2, 0, near)

        alpha_first(c)

        @pl.when(c == chunks - 1)
        def _():
            loop(chunks - 1)(alpha_second)

        add_first(c)
        relay_first(c)

    alpha_second(chunks - 1)

    @loop((chunks - early) * chunks)
    def _(i):
        alpha_piece(early + lax.div(i, chunks), lax.rem(i, chunks), 0, near)

    def send_far(r):
        loop(chunks)(lambda c: alpha_piece(r, c, near, shards))

    for c in range(max(0, chunks - 2), chunks):
        sum_sent(c, r1_send)
    for c in range(chunks):
        handed_first(c, g1_send, range(1, op_size))
    q_copy.wait()

    def row_block(r):
        return pl.ds(pl.multiple_of(r * block, block), block)

    def beta_second(r):
        slot = lax.rem(r, 2)
        at = row_block(r)
        wait(wrecv.at[r], w_recv.at[r])

        @pl.when(jnp.logical_and(r >= early, r + 1 < chunks))
        def _():
            send_far(r + 1)

        for c in range(chunks):
            keep(me * chunks + c, ysend[c, 0, at])

        @loop(shards, 1)
        def _(d):
            for c in range(chunks):
                keep(peer(d) * chunks + c, wrecv[r, c, d - 1])

        @pl.when(r >= 2)
        def _():
            sum_sent(r - 2, r2_send)

        group = math.gcd(share, 4)

        @loop(blocks // group)
        def _(i):
            for g in range(group):
                b = i * group + g
                here = pl.ds(pl.multiple_of(lax.rem(b, share) * block, block), block)
                part[slot, mate(lax.div(b, share)), here] = scale * beta(small, b, block)

        send_stage(slot, r, 0, r2_send, r2_recv)

        @pl.when(r == 0)
        def _():
            if early < chunks:
                send_far(early)


    def out_part(r, p, q):
        lo, n = cuts(block)[p]
        here = pl.ds(pl.multiple_of(r * block + lo, 8), n)
        return out_hbm.at[here, pl.ds(pl.multiple_of(mate(q) * segment, segment), segment)]

    def hand_second(r, p, source, q, across):
        lo, n = cuts(block)[p]
        own = vq.at[pl.ds(pl.multiple_of(r * block + lo, 8), n)]
        there = out_part(r, p, source)
        to_mate(
            there if source else own, there,
            g2_send.at[r, q - 1, p], g2_recv.at[r, q - 1, p], across,
        )

    def add_second(r):
        slot = lax.rem(r, 2)
        at = row_block(r)
        arrived(slot, r, bits - 1, r2_recv)
        for j in range(share):
            columns = pl.ds(j * block, block)
            vq[at, columns] = own_total(slot, j * block, block) - vq[at, columns]
        hand_out(r, hand_second, waves[0])
        pltpu.make_async_copy(vq.at[at], out_hbm.at[at, quarter], o_sem.at[r]).start()

    def handed_second(r, sem, slots_):
        for p in range(bits):
            for q in slots_:
                wait(out_part(r, p, q), sem.at[r, q - 1, p])

    def relay_second(r):
        for wave in waves[1:-1]:
            handed_second(r, g2_recv, wave)
            hand_out(r, hand_second, wave)

    acts = {
        "beta": beta_second,
        "relay": lambda r: relay_stages(lax.rem(r, 2), r, r2_send, r2_recv),
        "add": add_second,
        "hand": relay_second,
    }
    order = [(act, r) for r in range(min(2, chunks)) for act in ("beta", "relay")]
    order += [(act, r) for act in ("add", "hand") for r in range(min(2, chunks))]
    for r in range(2, chunks):
        order.insert(len(order) - (r == 2), ("beta", r))
        order += [(act, r) for act in ("relay", "add", "hand")]

    @loop(len(order))
    def _(t):
        for name, act in acts.items():
            ticks = [order.index((name, r)) for r in range(chunks)]
            now = functools.reduce(jnp.logical_or, [t == k for k in ticks])
            r = sum(jnp.minimum(jnp.maximum(t - k + 1, 0), 1) for k in ticks) - 1

            @pl.when(now)
            def _():
                act(r)

    for r in range(chunks):
        handed_second(r, g2_recv, waves[-1])
        handed_second(r, g2_send, range(1, op_size))
        wait(vq.at[pl.ds(r * block, block)], o_sem.at[r])
        wait(wrecv.at[r], w_send.at[r])
        wait(precv.at[r, pl.ds(1, shards - 1)], p_send.at[r])
    for r in range(max(0, chunks - 2), chunks):
        sum_sent(r, r2_send)


def per_device(coeffs, previous, block_values, block_cols):
    op_size, shards = lax.axis_size("op"), lax.axis_size("str")
    scale = 2.0 / math.sqrt(block_values.shape[0] * op_size)
    values = block_values[0]
    cols = block_cols[0].reshape(-1)
    blocks, slots, block, _ = values.shape
    rows, width = coeffs.shape
    chunks = blocks // shards
    piece = rows // op_size
    segment = width // op_size
    paths = (chunks, op_size - 1, max(1, op_size.bit_length() - 1))
    vmem, dma = pltpu.VMEM, pltpu.SemaphoreType.DMA
    anywhere = pl.BlockSpec(memory_space=pl.ANY)
    return pl.pallas_call(
        functools.partial(body, shards, op_size, slots, block, chunks, scale),
        out_shape=jax.ShapeDtypeStruct((rows, width), F32),
        in_specs=[pl.BlockSpec(memory_space=pltpu.SMEM), anywhere, anywhere, anywhere],
        out_specs=anywhere,
        scratch_shapes=[
            vmem((blocks, slots, block, block), BF16),
            vmem((blocks, 2 * rows, block), BF16),
            vmem((chunks, shards, rows, block), F32),
            vmem((chunks, shards - 1, rows, block), F32),
            vmem((chunks, chunks, shards - 1, block, block), F32),
            vmem((chunks, shards, piece, block), F32),
            vmem((blocks, 2 * block, block), BF16),
            vmem((2, op_size, segment, block), F32),
            vmem((chunks, op_size, segment, block), F32),
            vmem((2, op_size - 1, segment, block), F32),
            vmem((2, rows, rows), F32),
            vmem((rows, segment), F32),
            dma, dma((2,)), dma, dma((chunks,)),
            dma((chunks,)), dma((chunks,)), dma((chunks,)), dma((chunks,)),
            dma(paths), dma(paths), dma(paths), dma(paths),
            dma((chunks,)), dma((chunks,)),
            dma(paths), dma(paths), dma(paths), dma(paths),
        ],
        compiler_params=pltpu.CompilerParams(
            collective_id=0, has_side_effects=True, vmem_limit_bytes=VMEM_LIMIT
        ),
        cost_estimate=pl.CostEstimate(
            flops=16 * blocks * slots * block * block * rows,
            bytes_accessed=32 * rows * width,
            transcendentals=0,
        ),
    )(cols, values, coeffs, previous)


def solution(mesh):
    placed = (P("str", None), P("str", None), P("op", None, None, None, None), P("op", None, None))
    return jax.shard_map(
        per_device, mesh=mesh, in_specs=placed, out_specs=P("str", None), check_vma=False
    )
```
